256 devices in a mesh: gx: 8 (over y_lo, x), gy: 32 (over y_hi, z, core).
Axes of the slice: x: 4, y: 4 (y_hi: 2, y_lo: 2; y = y_hi * 2 + y_lo), z: 8, core: 2. Of those that a mesh axis runs over, the one named last changes fastest.
Arguments:
- e_field: float32 [3, 128, 48, 4096], P(None, 'gx', None, 'gy'), may hold values from -6 to 6
- h_field: float32 [3, 128, 48, 4096], P(None, 'gx', None, 'gy'), may hold values from -6 to 6
- current: float32 [3, 128, 48, 4096], P(None, 'gx', None, 'gy'), may hold values from -3 to 3
- material: int32 [128, 48, 4096], P('gx', None, 'gy'), may hold values from 0 to 2
- pml_cells: int32 [2], replicated, may hold values from 8 to 16, as said below
- forward_field: bfloat16 [24, 128, 12, 4096], P(None, 'gx', None, 'gy'), may hold values from -2.5 to 2.5
- time_index: int32 [1], replicated, may hold values from 2 to 4095
Outputs:
- e_out: float32 [3, 128, 48, 4096], P(None, 'gx', None, 'gy')
- h_out: float32 [3, 128, 48, 4096], P(None, 'gx', None, 'gy')
- current_out: float32 [3, 128, 48, 4096], P(None, 'gx', None, 'gy')
- design_grad: float32 [128, 12, 4096], P('gx', None, 'gy')
The draws below stay inside these ranges and needn't reach their ends.
Inputs may be any that keep to these rules, and one draw needn't show every extreme that they name: `material`: 0 is air, 1 dielectric, 2 Drude metal. `pml_cells`: exactly one of the two thicknesses equals 16.
All inputs are finite; a program needn't handle non-finite values.
Results may differ from the reference program's by a relative error of at most 0.0003.
Values sent between devices are 32-bit elements; how exact they have to be, the bound alone decides.
A program may use at most 64 MiB of HBM per device.

```python
import math
import jax
import jax.numpy as jnp
from jax import lax

Z = 48
DZ = 12
PML_MAX = 16
FREQ = 4
STEPS = 2
Z0 = 18
NX = 128
NY = 4096


def draw_pml_cells(key, part):
    side_key, width_key = jax.random.split(jax.random.fold_in(key, 11))
    side_pick = jax.random.randint(side_key, (), 0, 2)
    other_width = jax.random.randint(width_key, (), PML_MAX // 2, PML_MAX)
    full_width = jnp.full((), PML_MAX, jnp.int32)
    low_width = jnp.where(side_pick == 0, full_width, other_width)
    high_width = jnp.where(side_pick == 0, other_width, full_width)
    return jnp.stack([low_width, high_width]).astype(jnp.int32)


def place_ends(result, key, least, top_value):
    index_at = [jax.random.randint(jax.random.fold_in(key, axis), (), 0, length) for axis, length in enumerate(result.shape)]
    main_axis = result.shape.index(max(result.shape))
    next_to = index_at[:main_axis] + [(index_at[main_axis] + 1) % result.shape[main_axis]] + index_at[main_axis + 1:]
    return result.at[tuple(index_at)].set(least).at[tuple(next_to)].set(top_value)


def shard_levels(key, shape, pieces, smallest, largest):
    loudness = 1.0
    for dim, shards_of in pieces:
        steps = jax.random.uniform(jax.random.fold_in(jax.random.fold_in(key, 6), dim), (shards_of,), jnp.float32, smallest / len(pieces), largest / len(pieces))
        loudness = loudness * jnp.repeat(jnp.exp(steps), shape[dim] // shards_of).reshape((-1,) + (1,) * (len(shape) - 1 - dim))
    return loudness


def normal_values(own_key, shape, width, limit, cuts=(), kind=jnp.bfloat16):
    values = width * jax.random.normal(own_key, shape, jnp.float32)
    if cuts:
        values = values * shard_levels(own_key, shape, cuts, -0.22, 0.18)
    return jnp.clip(values, -limit, limit).astype(kind)


def setup_inputs(seed: int = 0) -> dict:
    key_list = jax.random.split(jax.random.key(seed), 8)
    return {
        "e_field": normal_values(key_list[0], (3, NX, Z, NY), 1.0, 6.0, ((1, 8), (3, 32)), jnp.float32),
        "h_field": normal_values(key_list[1], (3, NX, Z, NY), 1.0, 6.0, ((1, 8), (3, 32)), jnp.float32),
        "current": normal_values(key_list[2], (3, NX, Z, NY), 0.5, 3.0, ((1, 8), (3, 32)), jnp.float32),
        "material": place_ends(jax.random.randint(key_list[3], (NX, Z, NY), 0, 3), jax.random.fold_in(key_list[3], 1), 0, 2).astype(jnp.int32),
        "pml_cells": draw_pml_cells(jax.random.fold_in(key_list[7], 71), 0),
        "forward_field": normal_values(key_list[5], (6 * FREQ, NX, DZ, NY), 0.35, 2.5, ((1, 8), (3, 32))),
        "time_index": jax.random.randint(key_list[6], (1,), 2, 4096).astype(jnp.int32),
    }


COURANT = 0.5
DIELECTRIC = 4.0
SIGMA_PEAK = 0.8
DRUDE_KEEP = 0.95 / 1.05
DRUDE_GAIN = 0.25 / 1.05
NUMERATORS = (3, 4, 5, 6)
PERIOD_STEPS = 64

def absorber(pml_cells, z_cells):
    z_index = jnp.arange(z_cells, dtype=jnp.int32)
    low_cells = pml_cells[0]
    high_cells = pml_cells[1]
    low_depth = jnp.maximum(low_cells - z_index, 0).astype(jnp.float32) / low_cells.astype(jnp.float32)
    high_depth = jnp.maximum(z_index - (z_cells - 1 - high_cells), 0).astype(jnp.float32) / high_cells.astype(jnp.float32)
    return (SIGMA_PEAK * (low_depth ** 3 + high_depth ** 3)).reshape((z_cells, 1))

def z_next(field_block):
    axis_id = field_block.ndim - 2
    extent = field_block.shape[axis_id]
    zero_plane = jnp.zeros_like(lax.slice_in_dim(field_block, 0, 1, axis=axis_id))
    return jnp.concatenate([lax.slice_in_dim(field_block, 1, extent, axis=axis_id), zero_plane], axis_id)

def z_prev(field_block):
    axis_id = field_block.ndim - 2
    extent = field_block.shape[axis_id]
    zero_plane = jnp.zeros_like(lax.slice_in_dim(field_block, 0, 1, axis=axis_id))
    return jnp.concatenate([zero_plane, lax.slice_in_dim(field_block, 0, extent - 1, axis=axis_id)], axis_id)

def h_update(h_now, e_now, next_vals, decay_z, h_scale):
    ey_xn, ez_xn, ex_yn, ez_yn = next_vals
    e_x, e_y, e_z = (e_now[0], e_now[1], e_now[2])
    curl_x = ez_yn - e_z - (z_next(e_y) - e_y)
    curl_y = z_next(e_x) - e_x - (ez_xn - e_z)
    curl_z = ey_xn - e_y - (ex_yn - e_x)
    return decay_z * h_now - h_scale * jnp.stack([curl_x, curl_y, curl_z])

def e_update(e_now, h_now, j_now, prev_vals, decay_z, e_scale, metal_mask):
    hy_xp, hz_xp, hx_yp, hz_yp = prev_vals
    h_x, h_y, h_z = (h_now[0], h_now[1], h_now[2])
    back_x = h_z - hz_yp - (h_y - z_prev(h_y))
    back_y = h_x - z_prev(h_x) - (h_z - hz_xp)
    back_z = h_y - hy_xp - (h_x - hx_yp)
    e_new = decay_z * e_now + e_scale * (jnp.stack([back_x, back_y, back_z]) - metal_mask * j_now)
    j_new = metal_mask * (DRUDE_KEEP * j_now + DRUDE_GAIN * e_new)
    return (e_new, j_new)

def phase_weights(forward_field, time_index):
    numerators = jnp.array(NUMERATORS, dtype=jnp.int32)
    levels = jnp.arange(STEPS, dtype=jnp.int32)
    tick_ids = time_index[0] - levels
    turn_ids = jnp.remainder(numerators[None, :] * tick_ids[:, None], PERIOD_STEPS)
    angles = turn_ids.astype(jnp.float32) * (2.0 * math.pi / PERIOD_STEPS)
    coeffs = jnp.stack([jnp.cos(angles), -jnp.sin(angles)], axis=-1)
    forward32 = forward_field.astype(jnp.float32).reshape((FREQ, 2, 3) + forward_field.shape[1:])
    return jnp.einsum('nfp,fpcxzy->ncxzy', coeffs, forward32, precision=lax.Precision.HIGHEST)

def level_grad(ex_centre, ey_centre, ez_centre, level_weights):
    return ex_centre * level_weights[0] + ey_centre * level_weights[1] + ez_centre * level_weights[2]

def reference(e_field, h_field, current, material, pml_cells, forward_field, time_index):
    sigma_z = absorber(pml_cells, Z)
    half_loss = 1.0 + 0.5 * sigma_z
    decay_z = (1.0 - 0.5 * sigma_z) / half_loss
    h_scale = COURANT / half_loss
    dielectric = (material == 1).astype(jnp.float32)
    metal_mask = (material == 2).astype(jnp.float32)
    e_scale = COURANT / ((1.0 + (DIELECTRIC - 1.0) * dielectric) * half_loss)
    weights = phase_weights(forward_field, time_index)
    grad_sum = jnp.zeros((NX, DZ, NY), jnp.float32)
    e_now, h_now, j_now = (e_field, h_field, current)
    for level_idx in range(STEPS):
        slab_e = e_now[:, :, Z0:Z0 + DZ, :]
        ex_centre = 0.5 * (slab_e[0] + jnp.roll(slab_e[0], -1, 0))
        ey_centre = 0.5 * (slab_e[1] + jnp.roll(slab_e[1], -1, 2))
        ez_centre = 0.5 * (slab_e[2] + e_now[2, :, Z0 + 1:Z0 + DZ + 1, :])
        grad_sum = grad_sum + level_grad(ex_centre, ey_centre, ez_centre, weights[level_idx])
        next_vals = (jnp.roll(e_now[1], -1, 0), jnp.roll(e_now[2], -1, 0), jnp.roll(e_now[0], -1, 2), jnp.roll(e_now[2], -1, 2))
        h_now = h_update(h_now, e_now, next_vals, decay_z, h_scale)
        prev_vals = (jnp.roll(h_now[1], 1, 0), jnp.roll(h_now[2], 1, 0), jnp.roll(h_now[0], 1, 2), jnp.roll(h_now[2], 1, 2))
        e_now, j_now = e_update(e_now, h_now, j_now, prev_vals, decay_z, e_scale, metal_mask)
    return (e_now, h_now, j_now, grad_sum)
```

```python
import functools
import math

import jax
import jax.numpy as jnp
from jax import lax
from jax.experimental import pallas as pl
from jax.experimental.pallas import tpu as pltpu
from jax.sharding import PartitionSpec as P

Z = 48
DZ = 12
FREQ = 4
STEPS = 2
Z0 = 18
W0 = 16
WN = 16
OFF = Z0 - W0
YL = 128
GAP = 16

COURANT = 0.5
SIGMA_PEAK = 0.8
DRUDE_KEEP = 0.95 / 1.05
DRUDE_GAIN = 0.25 / 1.05
PERIOD_STEPS = 64
F32 = jnp.float32
MESH = pl.DeviceIdType.MESH


def lanes():
    return lax.broadcasted_iota(jnp.int32, (Z, YL), 1)


def rows():
    return lax.broadcasted_iota(jnp.int32, (Z, YL), 0)


def z_next(v):
    return jnp.where(rows() == Z - 1, 0.0, pltpu.roll(v, Z - 1, 0))


def z_prev(v):
    return jnp.where(rows() == 0, 0.0, pltpu.roll(v, 1, 0))


def absorber(pml):
    low = pml[0]
    high = pml[1]
    z = rows()
    low_depth = jnp.maximum(low - z, 0).astype(F32) / low.astype(F32)
    high_depth = jnp.maximum(z - (Z - 1 - high), 0).astype(F32) / high.astype(F32)
    sigma = SIGMA_PEAK * (low_depth * low_depth * low_depth + high_depth * high_depth * high_depth)
    half_loss = 1.0 + 0.5 * sigma
    return (1.0 - 0.5 * sigma) / half_loss, COURANT / half_loss


def phase_table(tick):
    lane = lax.broadcasted_iota(jnp.int32, (8, YL), 1)
    level = lane // 8
    freq = (lane % 8) // 2
    turn = ((3 + freq) * (tick[0] - level)) & (PERIOD_STEPS - 1)
    angle = turn.astype(F32) * (2.0 * math.pi / PERIOD_STEPS)
    return jnp.where(lane % 2 == 0, jnp.cos(angle), -jnp.sin(angle))


def h_partial(x, e, h, h_out, decay, scale, packs):
    lane = lanes()
    ex, ey, ez = e[0, x], e[1, x], e[2, x]
    last = lane == YL - 1
    ez_yn = jnp.where(last, 0.0, pltpu.roll(ez, YL - 1, 1))
    ex_yn = jnp.where(last, 0.0, pltpu.roll(ex, YL - 1, 1))
    hx = decay * h[0, x] - scale * (ez_yn - ez - (z_next(ey) - ey))
    hy = decay * h[1, x] - scale * (z_next(ex) - ex - (e[2, x + 1] - ez))
    hz = decay * h[2, x] - scale * (e[1, x + 1] - ey - (ex_yn - ex))
    h_out[0, x] = hx
    h_out[1, x] = hy
    h_out[2, x] = hz
    first_cols, last_cols = packs
    for group, v in enumerate((ex, ez, ey)):
        at = GAP * group + x
        first_cols = jnp.where(lane == at, pltpu.roll(v, at, 1), first_cols)
    for group, v in enumerate((hx, hz)):
        at = GAP * group + x
        last_cols = jnp.where(lane == at, pltpu.roll(v, at + 1, 1), last_cols)
    return first_cols, last_cols


def rims(e, pack_e, in_x, in_y, diag_e, diag_h, scale):
    lane = lanes()
    hy = in_x[0] + scale * e[2, 0]
    corner = jnp.where(lane == YL - 1, pltpu.roll(diag_e, YL - GAP, 1), 0.0)
    hz = in_x[1] + scale * (corner - e[1, 0])
    term = jnp.where(
        lane < GAP,
        -pltpu.roll(pack_e, YL - GAP, 1),
        jnp.where(lane < 2 * GAP, pltpu.roll(pack_e, GAP, 1), 0.0),
    )
    return hy, hz, in_y, term


def e_update(x, prev, hp, e, j, mat, col_e, col_h, decay, scale, outs):
    lane = lanes()
    e_out, h_out, j_out = outs
    hy_xp, hz_xp = prev
    last = lane == YL - 1
    first = lane == 0
    ex_halo = pltpu.roll(col_e, YL - 1 - x, 1)
    ez_halo = pltpu.roll(col_e, YL - 1 - GAP - x, 1)
    hx = hp[0, x] - jnp.where(last, scale * ez_halo, 0.0)
    hy = hp[1, x]
    hz = hp[2, x] + jnp.where(last, scale * ex_halo, 0.0)
    h_out[0, x] = hx
    h_out[1, x] = hy
    h_out[2, x] = hz
    hx_yp = jnp.where(first, pltpu.roll(col_h, YL - x, 1), pltpu.roll(hx, 1, 1))
    hz_yp = jnp.where(first, pltpu.roll(col_h, YL - GAP - x, 1), pltpu.roll(hz, 1, 1))
    m = mat[x]
    metal = m == 2
    e_scale = scale * jnp.where(m == 1, 0.25, 1.0)
    backs = (
        hz - hz_yp - (hy - z_prev(hy)),
        hx - z_prev(hx) - (hz - hz_xp),
        hy - hy_xp - (hx - hx_yp),
    )
    for c, back in enumerate(backs):
        j_now = j[c, x]
        e_new = decay * e[c, x] + e_scale * (back - jnp.where(metal, j_now, 0.0))
        e_out[c, x] = e_new
        j_out[c, x] = jnp.where(metal, DRUDE_KEEP * j_now + DRUDE_GAIN * e_new, 0.0)
    return hy, hz


def window_grad(x, e, col_e, w, level):
    lane = lax.broadcasted_iota(jnp.int32, (WN, YL), 1)
    win = pl.ds(W0, WN)
    ex, ey, ez = e[0, x, win], e[1, x, win], e[2, x, win]
    ex_xn = e[0, x + 1, win]
    halo = pltpu.roll(col_e, YL - 1 - 2 * GAP - x, 1)
    ey_yn = jnp.where(lane == YL - 1, halo, pltpu.roll(ey, YL - 1, 1))
    ez_zn = e[2, x, pl.ds(W0 + 1, WN)]
    return 0.5 * (
        (ex + ex_xn) * w[level, 0, x] + (ey + ey_yn) * w[level, 1, x] + (ez + ez_zn) * w[level, 2, x]
    )


def exchange_kernel(
    gx, gy, nx,
    pml, tick, e_in, h_in, j_in, m_in, f_in,
    e1, h1, j1, mat, w, grad, coef, rim_x, col_e_out, col_h_out,
    e0, hp, j0, fwd, pack_e, pack_h, send_h, got_e, got_slab, got_h, got_ye, got_yh, got_de, got_dh,
    load_sem, send_sem, recv_sem,
):
    me_x = lax.axis_index("gx")
    me_y = lax.axis_index("gy")
    x_next, x_prev = lax.rem(me_x + 1, gx), lax.rem(me_x + gx - 1, gx)
    y_next, y_prev = lax.rem(me_y + 1, gy), lax.rem(me_y + gy - 1, gy)
    barrier = pltpu.get_barrier_semaphore()
    peers = (
        (x_prev, me_y), (x_next, me_y), (me_x, y_prev), (me_x, y_next), (x_next, y_prev), (x_prev, y_next),
    )
    for peer in peers:
        pl.semaphore_signal(barrier, inc=1, device_id=peer, device_id_type=MESH)

    loads = [
        pltpu.make_async_copy(e_in, e0.at[:, pl.ds(0, nx)], load_sem.at[0]),
        pltpu.make_async_copy(h_in, hp, load_sem.at[1]),
        pltpu.make_async_copy(f_in, fwd, load_sem.at[2]),
        pltpu.make_async_copy(j_in, j0, load_sem.at[3]),
        pltpu.make_async_copy(m_in, mat, load_sem.at[4]),
    ]
    for load in loads:
        load.start()

    lane = lanes()
    decay, scale = absorber(pml)
    coef[0] = decay
    coef[1] = scale
    zero = jnp.zeros((Z, YL), F32)
    for c in range(3):
        e0[c, nx] = zero
        e1[c, nx] = zero

    def send(level, e):
        routes = (
            (e.at[pl.ds(1, 2), 0], got_e.at[level]),
            (e.at[0, 0, pl.ds(W0, WN)], got_slab.at[level]),
            (send_h.at[level], got_h.at[level]),
            (pack_e.at[level], got_ye.at[level]),
            (pack_h.at[level], got_yh.at[level]),
            (pack_e.at[level], got_de.at[level]),
            (pack_h.at[level], got_dh.at[level]),
        )
        targets = (peers[0], peers[0], peers[1], peers[2], peers[3], peers[4], peers[5])
        copies = []
        for i, ((src, dst), peer) in enumerate(zip(routes, targets)):
            copies.append(
                pltpu.make_async_remote_copy(
                    src_ref=src,
                    dst_ref=dst,
                    send_sem=send_sem.at[level, i],
                    recv_sem=recv_sem.at[level, i],
                    device_id=peer,
                    device_id_type=MESH,
                )
            )
        for copy in copies:
            copy.start()
        return copies

    def prepare(level, e, h, h_out):
        def plane(x, packs):
            return h_partial(x, e, h, h_out, coef[0], coef[1], packs)

        first_cols, last_cols = lax.fori_loop(0, nx, plane, (zero, zero))
        last_cols = jnp.where(lane == 2 * GAP, pltpu.roll(e[1, 0], 2 * GAP + 1, 1), last_cols)
        pack_e[level] = first_cols
        pack_h[level] = last_cols
        send_h[level, 0] = h_out[1, nx - 1]
        send_h[level, 1] = h_out[2, nx - 1]

    def receive(level, e, h):
        e[0, nx, pl.ds(W0, WN)] = got_slab[level]
        h[1, nx - 1] = h[1, nx - 1] + scale * got_e[level, 1]
        h[2, nx - 1] = h[2, nx - 1] - scale * got_e[level, 0]
        corner = jnp.where(lane == YL - 1, pltpu.roll(got_de[level], YL - nx, 1), 0.0)
        hy = got_h[level, 0] + scale * e[2, 0]
        hz = got_h[level, 1] + scale * (corner - e[1, 0])
        own = pack_e[level]
        term = jnp.where(
            lane < GAP,
            -pltpu.roll(own, YL - GAP, 1),
            jnp.where(lane < 2 * GAP, pltpu.roll(own, GAP, 1), 0.0),
        )
        far = pltpu.roll(got_dh[level], YL + (GAP + nx - 1) - 2 * GAP, 1)
        term = term - jnp.where(lane == GAP + nx - 1, far, 0.0)
        return hy, hz, got_ye[level], got_yh[level] + scale * term

    loads[0].wait()
    loads[1].wait()
    prepare(0, e0, hp, hp)
    pl.semaphore_wait(barrier, len(peers))
    copies = send(0, e0)

    loads[2].wait()
    table = phase_table(tick)
    terms = [
        [jnp.broadcast_to(table[0:1, n * 8 + k : n * 8 + k + 1], (DZ, YL)) for k in range(8)]
        for n in range(STEPS)
    ]

    def weigh(x, carry):
        for c in range(3):
            sums = [None, None]
            for k in range(8):
                value = fwd[k * 3 + c, x].astype(F32)
                for n in range(STEPS):
                    part = terms[n][k] * value
                    sums[n] = part if sums[n] is None else sums[n] + part
            for n in range(STEPS):
                w[n, c, x, pl.ds(OFF, DZ)] = sums[n]
        return carry

    lax.fori_loop(0, nx, weigh, 0)
    loads[3].wait()
    loads[4].wait()
    for copy in copies:
        copy.wait()

    hy, hz, col_e, col_h = receive(0, e0, hp)
    col_e_out[...] = col_e
    col_h_out[...] = col_h

    def advance(x, prev):
        return e_update(
            x, prev, hp, e0, j0, mat, col_e_out[...], col_h_out[...], coef[0], coef[1], (e1, hp, j1)
        )

    lax.fori_loop(0, nx, advance, (hy, hz))
    prepare(1, e1, hp, h1)
    copies = send(1, e1)

    col_slab = got_ye[0, pl.ds(W0, WN)]

    def level_grad(x, carry):
        grad[x] = window_grad(x, e0, col_slab, w, 0)
        return carry

    lax.fori_loop(0, nx, level_grad, 0)
    for copy in copies:
        copy.wait()
    hy, hz, col_e, col_h = receive(1, e1, h1)
    rim_x[0] = hy
    rim_x[1] = hz
    col_e_out[...] = col_e
    col_h_out[...] = col_h


def finish_kernel(
    nx,
    e1, h1, j1, mat, w, grad, coef, rim_x, col_e, col_h,
    e_res, h_res, j_res, g_res,
    e2, h2, j2, g2, sem, g_sem,
):
    def copies(x):
        return [
            pltpu.make_async_copy(src.at[:, x], dst.at[:, x], sem.at[i, x])
            for i, (src, dst) in enumerate(((e2, e_res), (h2, h_res), (j2, j_res)))
        ]

    def advance(x, prev):
        out = e_update(
            x, prev, h1, e1, j1, mat, col_e[...], col_h[...], coef[0], coef[1], (e2, h2, j2)
        )
        for copy in copies(x):
            copy.start()
        return out

    def level_grad(x, carry):
        total = grad[x] + window_grad(x, e1, col_e[pl.ds(W0, WN)], w, 1)
        g2[x] = total[OFF : OFF + DZ]
        return carry

    lax.fori_loop(0, nx, advance, (rim_x[0], rim_x[1]))
    lax.fori_loop(0, nx, level_grad, 0)
    g_copy = pltpu.make_async_copy(g2, g_res, g_sem)
    g_copy.start()

    def drain(x, carry):
        for copy in copies(x):
            copy.wait()
        return carry

    lax.fori_loop(0, nx, drain, 0)
    g_copy.wait()


def body(gx, gy, e_field, h_field, current, material, pml_cells, forward_field, time_index):
    nx = e_field.shape[1]
    field = (3, nx, Z, YL)
    padded = (3, nx + 1, Z, YL)
    plane = (Z, YL)
    any_spec = pl.BlockSpec(memory_space=pl.ANY)
    smem = pl.BlockSpec(memory_space=pltpu.SMEM)
    vmem = pl.BlockSpec(memory_space=pltpu.VMEM)
    kept = [
        (padded, F32), (field, F32), (field, F32), ((nx, Z, YL), jnp.int32), ((STEPS, 3, nx, WN, YL), F32),
        ((nx, WN, YL), F32), ((2,) + plane, F32), ((2,) + plane, F32), (plane, F32), (plane, F32),
    ]
    mid = pl.pallas_call(
        functools.partial(exchange_kernel, gx, gy, nx),
        out_shape=[pltpu.VMEM(shape, dtype) for shape, dtype in kept],
        in_specs=[smem, smem] + [any_spec] * 5,
        out_specs=[vmem] * len(kept),
        scratch_shapes=[
            pltpu.VMEM(padded, F32),
            pltpu.VMEM(field, F32),
            pltpu.VMEM(field, F32),
            pltpu.VMEM(forward_field.shape, forward_field.dtype),
            pltpu.VMEM((STEPS,) + plane, F32),
            pltpu.VMEM((STEPS,) + plane, F32),
            pltpu.VMEM((STEPS, 2) + plane, F32),
            pltpu.VMEM((STEPS, 2) + plane, F32),
            pltpu.VMEM((STEPS, WN, YL), F32),
            pltpu.VMEM((STEPS, 2) + plane, F32),
            pltpu.VMEM((STEPS,) + plane, F32),
            pltpu.VMEM((STEPS,) + plane, F32),
            pltpu.VMEM((STEPS,) + plane, F32),
            pltpu.VMEM((STEPS,) + plane, F32),
            pltpu.SemaphoreType.DMA((5,)),
            pltpu.SemaphoreType.DMA((STEPS, 7)),
            pltpu.SemaphoreType.DMA((STEPS, 7)),
        ],
        compiler_params=pltpu.CompilerParams(
            collective_id=0, has_side_effects=True, vmem_limit_bytes=24 << 20
        ),
        name="exchange",
    )(pml_cells, time_index, e_field, h_field, current, material, forward_field)
    return pl.pallas_call(
        functools.partial(finish_kernel, nx),
        out_shape=[
            jax.ShapeDtypeStruct(field, F32),
            jax.ShapeDtypeStruct(field, F32),
            jax.ShapeDtypeStruct(field, F32),
            jax.ShapeDtypeStruct((nx, DZ, YL), F32),
        ],
        in_specs=[vmem] * len(kept),
        out_specs=[any_spec] * 4,
        scratch_shapes=[
            pltpu.VMEM(field, F32),
            pltpu.VMEM(field, F32),
            pltpu.VMEM(field, F32),
            pltpu.VMEM((nx, DZ, YL), F32),
            pltpu.SemaphoreType.DMA((3, nx)),
            pltpu.SemaphoreType.DMA(()),
        ],
        compiler_params=pltpu.CompilerParams(vmem_limit_bytes=24 << 20),
        name="finish",
    )(*mid)


def solution(mesh):
    field = P(None, "gx", None, "gy")
    cell = P("gx", None, "gy")
    return jax.shard_map(
        functools.partial(body, mesh.shape["gx"], mesh.shape["gy"]),
        mesh=mesh,
        in_specs=(field, field, field, cell, P(), field, P()),
        out_specs=(field, field, field, cell),
        check_vma=False,
    )
```

```python
import functools
import math

import jax
import jax.numpy as jnp
from jax import lax
from jax.experimental import pallas as pl
from jax.experimental.pallas import tpu as pltpu
from jax.sharding import PartitionSpec as P

Z = 48
DZ = 12
FREQ = 4
STEPS = 2
Z0 = 18
W0 = 16
WN = 16
YL = 128
CHUNKS = 4
GAP = 16

COURANT = 0.5
SIGMA_PEAK = 0.8
DRUDE_KEEP = 0.95 / 1.05
DRUDE_GAIN = 0.25 / 1.05
PERIOD_STEPS = 64
F32 = jnp.float32
MESH = pl.DeviceIdType.MESH


def lanes():
    return lax.broadcasted_iota(jnp.int32, (Z, YL), 1)


def rows():
    return lax.broadcasted_iota(jnp.int32, (Z, YL), 0)


def z_next(v):
    return jnp.where(rows() == Z - 1, 0.0, pltpu.roll(v, Z - 1, 0))


def z_prev(v):
    return jnp.where(rows() == 0, 0.0, pltpu.roll(v, 1, 0))


def absorber(pml):
    low = pml[0]
    high = pml[1]
    z = rows()
    low_depth = jnp.maximum(low - z, 0).astype(F32) / low.astype(F32)
    high_depth = jnp.maximum(z - (Z - 1 - high), 0).astype(F32) / high.astype(F32)
    sigma = SIGMA_PEAK * (low_depth * low_depth * low_depth + high_depth * high_depth * high_depth)
    half_loss = 1.0 + 0.5 * sigma
    return (1.0 - 0.5 * sigma) / half_loss, COURANT / half_loss


def phase_table(tick):
    lane = lax.broadcasted_iota(jnp.int32, (8, YL), 1)
    level = lane // 8
    freq = (lane % 8) // 2
    turn = ((3 + freq) * (tick[0] - level)) & (PERIOD_STEPS - 1)
    angle = turn.astype(F32) * (2.0 * math.pi / PERIOD_STEPS)
    return jnp.where(lane % 2 == 0, jnp.cos(angle), -jnp.sin(angle))


def h_partial(x, e, h, h_out, decay, scale, packs):
    lane = lanes()
    ex, ey, ez = e[0, x], e[1, x], e[2, x]
    last = lane == YL - 1
    ez_yn = jnp.where(last, 0.0, pltpu.roll(ez, YL - 1, 1))
    ex_yn = jnp.where(last, 0.0, pltpu.roll(ex, YL - 1, 1))
    hx = decay * h[0, x] - scale * (ez_yn - ez - (z_next(ey) - ey))
    hy = decay * h[1, x] - scale * (z_next(ex) - ex - (e[2, x + 1] - ez))
    hz = decay * h[2, x] - scale * (e[1, x + 1] - ey - (ex_yn - ex))
    h_out[0, x] = hx
    h_out[1, x] = hy
    h_out[2, x] = hz
    first_cols, last_cols = packs
    for group, v in enumerate((ex, ez, ey)):
        at = GAP * group + x
        first_cols = jnp.where(lane == at, pltpu.roll(v, at, 1), first_cols)
    for group, v in enumerate((hx, hz)):
        at = GAP * group + x
        last_cols = jnp.where(lane == at, pltpu.roll(v, at + 1, 1), last_cols)
    return first_cols, last_cols


def column_to_tile(column):
    row = jnp.sum(jnp.where(lanes() == rows(), column, 0.0), axis=0, keepdims=True)
    return jnp.broadcast_to(row, (8, YL))


def tile_to_column(tile):
    return jnp.sum(jnp.where(lanes() == rows(), tile[0:1], 0.0), axis=1, keepdims=True)


def h_full(x, hp, col_e, scale):
    last = lanes() == YL - 1
    ex_halo = pltpu.roll(col_e, YL - 1 - x, 1)
    ez_halo = pltpu.roll(col_e, YL - 1 - GAP - x, 1)
    hx = hp[0, x] - jnp.where(last, scale * ez_halo, 0.0)
    hz = hp[2, x] + jnp.where(last, scale * ex_halo, 0.0)
    return hx, hp[1, x], hz


def e_update(x, prev, hp, e, j, mat, col_e, col_h, decay, scale, outs):
    lane = lanes()
    e_out, h_out, j_out = outs
    hy_xp, hz_xp = prev
    first = lane == 0
    hx, hy, hz = h_full(x, hp, col_e, scale)
    h_out[0, x] = hx
    h_out[1, x] = hy
    h_out[2, x] = hz
    hx_yp = jnp.where(first, pltpu.roll(col_h, YL - x, 1), pltpu.roll(hx, 1, 1))
    hz_yp = jnp.where(first, pltpu.roll(col_h, YL - GAP - x, 1), pltpu.roll(hz, 1, 1))
    m = mat[x]
    metal = m == 2
    e_scale = scale * jnp.where(m == 1, 0.25, 1.0)
    backs = (
        hz - hz_yp - (hy - z_prev(hy)),
        hx - z_prev(hx) - (hz - hz_xp),
        hy - hy_xp - (hx - hx_yp),
    )
    for c, back in enumerate(backs):
        j_now = j[c, x]
        e_new = decay * e[c, x] + e_scale * (back - jnp.where(metal, j_now, 0.0))
        e_out[c, x] = e_new
        j_out[c, x] = jnp.where(metal, DRUDE_KEEP * j_now + DRUDE_GAIN * e_new, 0.0)
    return hy, hz


def slab_grad(z, e, col_e, w, level):
    nx = e.shape[1] - 1
    lane = lax.broadcasted_iota(jnp.int32, (nx, YL), 1)
    sub = lax.broadcasted_iota(jnp.int32, (nx, YL), 0)

    def cells(c, x, k):
        return e[c, pl.ds(x, nx), k]

    k = Z0 + z
    ex, ey, ez = cells(0, 0, k), cells(1, 0, k), cells(2, 0, k)
    ex_xn, ez_zn = cells(0, 1, k), cells(2, 0, k + 1)
    halo = jnp.sum(jnp.where(lane == 2 * GAP + sub, col_e[k : k + 1], 0.0), axis=1, keepdims=True)
    ey_yn = jnp.where(lane == YL - 1, halo, pltpu.roll(ey, YL - 1, 1))
    return 0.5 * (
        (ex + ex_xn) * w[level, 0, z] + (ey + ey_yn) * w[level, 1, z] + (ez + ez_zn) * w[level, 2, z]
    )


def exchange_kernel(
    gx, gy, nx,
    pml_in, tick_in, e_in, h_in, j_in, m_in, f_in,
    e1, h1, j1, mat, w, grad, coef, rim_x, col_e_out, col_h_out,
    pml, tick, e0, hp, j0, fwd, pack_e, pack_h, send_h, tile_e, tile_h,
    got_e, got_slab, got_h, got_ye, got_yh, got_de, got_dh,
    field_sem, load_sem, send_sem, recv_sem,
):
    me_x = lax.axis_index("gx")
    me_y = lax.axis_index("gy")
    x_next, x_prev = lax.rem(me_x + 1, gx), lax.rem(me_x + gx - 1, gx)
    y_next, y_prev = lax.rem(me_y + 1, gy), lax.rem(me_y + gy - 1, gy)
    barrier = pltpu.get_barrier_semaphore()
    peers = (
        (x_prev, me_y), (x_next, me_y), (me_x, y_prev), (me_x, y_next), (x_next, y_prev), (x_prev, y_next),
    )
    for peer in peers:
        pl.semaphore_signal(barrier, inc=1, device_id=peer, device_id_type=MESH)

    small = [
        pltpu.make_async_copy(pml_in, pml, load_sem.at[3]),
        pltpu.make_async_copy(tick_in, tick, load_sem.at[4]),
    ]
    fields = []
    for i in reversed(range(CHUNKS)):
        span = pl.ds(i * nx // CHUNKS, nx // CHUNKS)
        fields.append(
            [
                pltpu.make_async_copy(e_in.at[:, span], e0.at[:, span], field_sem.at[0, i]),
                pltpu.make_async_copy(h_in.at[:, span], hp.at[:, span], field_sem.at[1, i]),
            ]
        )
    late = [
        pltpu.make_async_copy(f_in, fwd, load_sem.at[0]),
        pltpu.make_async_copy(j_in, j0, load_sem.at[1]),
        pltpu.make_async_copy(m_in, mat, load_sem.at[2]),
    ]
    for load in small + sum(fields, []) + late:
        load.start()
    for load in small:
        load.wait()

    lane = lanes()
    decay, scale = absorber(pml)
    coef[0] = decay
    coef[1] = scale
    zero = jnp.zeros((Z, YL), F32)
    for c in range(3):
        e0[c, nx] = zero
        e1[c, nx] = zero

    def route(level, i, e):
        src, dst, peer = (
            (e.at[pl.ds(1, 2), 0], got_e, 0),
            (e.at[0, 0, pl.ds(W0, WN)], got_slab, 0),
            (send_h.at[level], got_h, 1),
            (pack_e.at[level], got_ye, 2),
            (pack_h.at[level], got_yh, 3),
            (tile_e.at[level], got_de, 4),
            (tile_h.at[level], got_dh, 5),
        )[i]
        return pltpu.make_async_remote_copy(
            src_ref=src,
            dst_ref=dst.at[level],
            send_sem=send_sem.at[level, i],
            recv_sem=recv_sem.at[level, i],
            device_id=peers[peer],
            device_id_type=MESH,
        )

    def send(level, e, which):
        copies = [route(level, i, e) for i in which]
        for copy in copies:
            copy.start()
        return copies

    def last_plane(level, e, h, h_out):
        packs = h_partial(nx - 1, e, h, h_out, coef[0], coef[1], (zero, zero))
        send_h[level, 0] = h_out[1, nx - 1]
        send_h[level, 1] = h_out[2, nx - 1]
        tile_h[level] = column_to_tile(e[1, 0, :, YL - 1 : YL])
        tile_e[level] = column_to_tile(e[0, nx - 1, :, 0:1])
        return packs

    def receive(level, e, h):
        e[0, nx, pl.ds(W0, WN)] = got_slab[level]
        h[1, nx - 1] = h[1, nx - 1] + scale * got_e[level, 1]
        h[2, nx - 1] = h[2, nx - 1] - scale * got_e[level, 0]
        corner = jnp.where(lane == YL - 1, tile_to_column(got_de[level]), 0.0)
        hy = got_h[level, 0] + scale * e[2, 0]
        hz = got_h[level, 1] + scale * (corner - e[1, 0])
        own = pack_e[level]
        term = jnp.where(
            lane < GAP,
            -pltpu.roll(own, YL - GAP, 1),
            jnp.where(lane < 2 * GAP, pltpu.roll(own, GAP, 1), 0.0),
        )
        term = term - jnp.where(lane == GAP + nx - 1, tile_to_column(got_dh[level]), 0.0)
        return hy, hz, got_ye[level], got_yh[level] + scale * term

    def plane(step, packs, e, h, h_out):
        return h_partial(nx - 2 - step, e, h, h_out, coef[0], coef[1], packs)

    packs = None
    for i, parts in enumerate(fields):
        for load in parts:
            load.wait()
        if i == 0:
            head = functools.partial(h_partial, nx - 1, e0, hp, hp, decay, scale)
            packs = head((zero, zero))
        size = nx // CHUNKS
        packs = lax.fori_loop(
            max(i * size - 1, 0),
            (i + 1) * size - 1,
            functools.partial(plane, e=e0, h=hp, h_out=hp),
            packs,
        )
    pack_e[0] = packs[0]
    pack_h[0] = packs[1]
    send_h[0, 0] = hp[1, nx - 1]
    send_h[0, 1] = hp[2, nx - 1]
    tile_h[0] = column_to_tile(e0[1, 0, :, YL - 1 : YL])
    tile_e[0] = column_to_tile(e0[0, nx - 1, :, 0:1])
    pl.semaphore_wait(barrier, len(peers))
    copies = send(0, e0, (5, 4, 3, 2, 0, 1, 6))

    late[0].wait()
    table = phase_table(tick)
    terms = [
        [jnp.broadcast_to(table[0:1, n * 8 + k : n * 8 + k + 1], (nx, YL)) for k in range(8)]
        for n in range(STEPS)
    ]

    def weigh(z, carry):
        for c in range(3):
            sums = [None, None]
            for k in range(8):
                value = fwd[k * 3 + c, z].astype(F32)
                for n in range(STEPS):
                    part = terms[n][k] * value
                    sums[n] = part if sums[n] is None else sums[n] + part
            for n in range(STEPS):
                w[n, c, z] = sums[n]
        return carry

    lax.fori_loop(0, DZ, weigh, 0)
    late[1].wait()
    late[2].wait()
    for copy in copies:
        copy.wait()

    hy, hz, col_e, col_h = receive(0, e0, hp)
    col_e_out[...] = col_e
    col_h_out[...] = col_h

    def advance(x, prev):
        return e_update(
            x, prev, hp, e0, j0, mat, col_e_out[...], col_h_out[...], coef[0], coef[1], (e1, hp, j1)
        )

    prev = advance(0, (hy, hz))
    copies = send(1, e1, (0, 1))
    advance(nx - 1, h_full(nx - 2, hp, col_e_out[...], coef[1])[1:])
    packs = last_plane(1, e1, hp, h1)
    copies += send(1, e1, (2, 5, 6))
    lax.fori_loop(1, nx - 1, advance, prev)
    packs = lax.fori_loop(0, nx - 1, functools.partial(plane, e=e1, h=hp, h_out=h1), packs)
    pack_e[1] = packs[0]
    pack_h[1] = packs[1]
    copies += send(1, e1, (3, 4))

    for z in range(DZ):
        grad[z] = slab_grad(z, e0, got_ye.at[0], w, 0)
    for copy in copies:
        copy.wait()
    hy, hz, col_e, col_h = receive(1, e1, h1)
    rim_x[0] = hy
    rim_x[1] = hz
    col_e_out[...] = col_e
    col_h_out[...] = col_h


def finish_kernel(
    nx,
    e1, h1, j1, mat, w, grad, coef, rim_x, col_e, col_h,
    e_res, h_res, j_res, g_res,
    e2, h2, j2, g2, sem, g_sem,
):
    def copies(x):
        return [
            pltpu.make_async_copy(src.at[:, x], dst.at[:, x], sem.at[i, x])
            for i, (src, dst) in enumerate(((e2, e_res), (h2, h_res), (j2, j_res)))
        ]

    def advance(x, prev):
        out = e_update(
            x, prev, h1, e1, j1, mat, col_e[...], col_h[...], coef[0], coef[1], (e2, h2, j2)
        )
        for copy in copies(x):
            copy.start()
        return out

    lax.fori_loop(0, nx, advance, (rim_x[0], rim_x[1]))
    for z in range(DZ):
        g2[z] = grad[z] + slab_grad(z, e1, col_e, w, 1)
    g_copy = pltpu.make_async_copy(g2, g_res, g_sem)
    g_copy.start()

    def drain(x, carry):
        for copy in copies(x):
            copy.wait()
        return carry

    lax.fori_loop(0, nx, drain, 0)
    g_copy.wait()


def body(gx, gy, e_field, h_field, current, material, pml_cells, forward_field, time_index):
    nx = e_field.shape[1]
    slab = jnp.transpose(forward_field, (0, 2, 1, 3))
    field = (3, nx, Z, YL)
    padded = (3, nx + 1, Z, YL)
    plane = (Z, YL)
    any_spec = pl.BlockSpec(memory_space=pl.ANY)
    hbm = pl.BlockSpec(memory_space=pltpu.HBM)
    vmem = pl.BlockSpec(memory_space=pltpu.VMEM)
    kept = [
        (padded, F32), (field, F32), (field, F32), ((nx, Z, YL), jnp.int32), ((STEPS, 3, DZ, nx, YL), F32),
        ((DZ, nx, YL), F32), ((2,) + plane, F32), ((2,) + plane, F32), (plane, F32), (plane, F32),
    ]
    mid = pl.pallas_call(
        functools.partial(exchange_kernel, gx, gy, nx),
        out_shape=[pltpu.VMEM(shape, dtype) for shape, dtype in kept],
        in_specs=[hbm] * 7,
        out_specs=[vmem] * len(kept),
        scratch_shapes=[
            pltpu.SMEM((2,), jnp.int32),
            pltpu.SMEM((1,), jnp.int32),
            pltpu.VMEM(padded, F32),
            pltpu.VMEM(field, F32),
            pltpu.VMEM(field, F32),
            pltpu.VMEM(slab.shape, slab.dtype),
            pltpu.VMEM((STEPS,) + plane, F32),
            pltpu.VMEM((STEPS,) + plane, F32),
            pltpu.VMEM((STEPS, 2) + plane, F32),
            pltpu.VMEM((STEPS, 8, YL), F32),
            pltpu.VMEM((STEPS, 8, YL), F32),
            pltpu.VMEM((STEPS, 2) + plane, F32),
            pltpu.VMEM((STEPS, WN, YL), F32),
            pltpu.VMEM((STEPS, 2) + plane, F32),
            pltpu.VMEM((STEPS,) + plane, F32),
            pltpu.VMEM((STEPS,) + plane, F32),
            pltpu.VMEM((STEPS, 8, YL), F32),
            pltpu.VMEM((STEPS, 8, YL), F32),
            pltpu.SemaphoreType.DMA((2, CHUNKS)),
            pltpu.SemaphoreType.DMA((5,)),
            pltpu.SemaphoreType.DMA((STEPS, 7)),
            pltpu.SemaphoreType.DMA((STEPS, 7)),
        ],
        compiler_params=pltpu.CompilerParams(
            collective_id=0, has_side_effects=True, vmem_limit_bytes=58 << 20
        ),
        name="exchange",
    )(pml_cells, time_index, e_field, h_field, current, material, slab)
    e, h, j, grad = pl.pallas_call(
        functools.partial(finish_kernel, nx),
        out_shape=[
            jax.ShapeDtypeStruct(field, F32),
            jax.ShapeDtypeStruct(field, F32),
            jax.ShapeDtypeStruct(field, F32),
            jax.ShapeDtypeStruct((DZ, nx, YL), F32),
        ],
        in_specs=[vmem] * len(kept),
        out_specs=[any_spec] * 4,
        scratch_shapes=[
            pltpu.VMEM(field, F32),
            pltpu.VMEM(field, F32),
            pltpu.VMEM(field, F32),
            pltpu.VMEM((DZ, nx, YL), F32),
            pltpu.SemaphoreType.DMA((3, nx)),
            pltpu.SemaphoreType.DMA(()),
        ],
        compiler_params=pltpu.CompilerParams(vmem_limit_bytes=24 << 20),
        name="finish",
    )(*mid)
    return e, h, j, jnp.transpose(grad, (1, 0, 2))


def solution(mesh):
    field = P(None, "gx", None, "gy")
    cell = P("gx", None, "gy")
    return jax.shard_map(
        functools.partial(body, mesh.shape["gx"], mesh.shape["gy"]),
        mesh=mesh,
        in_specs=(field, field, field, cell, P(), field, P()),
        out_specs=(field, field, field, cell),
        check_vma=False,
    )
```

```python
import functools
import math

import jax
import jax.numpy as jnp
from jax import lax
from jax.experimental import pallas as pl
from jax.experimental.pallas import tpu as pltpu
from jax.sharding import PartitionSpec as P

Z = 48
DZ = 12
FREQ = 4
STEPS = 2
Z0 = 18
W0 = 16
WN = 16
YL = 128
CHUNKS = 4
GAP = 16

COURANT = 0.5
SIGMA_PEAK = 0.8
DRUDE_KEEP = 0.95 / 1.05
DRUDE_GAIN = 0.25 / 1.05
PERIOD_STEPS = 64
F32 = jnp.float32
MESH = pl.DeviceIdType.MESH


def lanes():
    return lax.broadcasted_iota(jnp.int32, (Z, YL), 1)


def rows():
    return lax.broadcasted_iota(jnp.int32, (Z, YL), 0)


def z_next(v):
    return jnp.where(rows() == Z - 1, 0.0, pltpu.roll(v, Z - 1, 0))


def z_prev(v):
    return jnp.where(rows() == 0, 0.0, pltpu.roll(v, 1, 0))


def absorber(pml):
    low = pml[0]
    high = pml[1]
    z = rows()
    low_depth = jnp.maximum(low - z, 0).astype(F32) / low.astype(F32)
    high_depth = jnp.maximum(z - (Z - 1 - high), 0).astype(F32) / high.astype(F32)
    sigma = SIGMA_PEAK * (low_depth * low_depth * low_depth + high_depth * high_depth * high_depth)
    half_loss = 1.0 + 0.5 * sigma
    return (1.0 - 0.5 * sigma) / half_loss, COURANT / half_loss


def phase_table(tick):
    lane = lax.broadcasted_iota(jnp.int32, (8, YL), 1)
    level = lane // 8
    freq = (lane % 8) // 2
    turn = ((3 + freq) * (tick[0] - level)) & (PERIOD_STEPS - 1)
    angle = turn.astype(F32) * (2.0 * math.pi / PERIOD_STEPS)
    return jnp.where(lane % 2 == 0, jnp.cos(angle), -jnp.sin(angle))


def h_partial(x, e, h, h_out, decay, scale, packs):
    lane = lanes()
    ex, ey, ez = e[0, x], e[1, x], e[2, x]
    last = lane == YL - 1
    ez_yn = jnp.where(last, 0.0, pltpu.roll(ez, YL - 1, 1))
    ex_yn = jnp.where(last, 0.0, pltpu.roll(ex, YL - 1, 1))
    hx = decay * h[0, x] - scale * (ez_yn - ez - (z_next(ey) - ey))
    hy = decay * h[1, x] - scale * (z_next(ex) - ex - (e[2, x + 1] - ez))
    hz = decay * h[2, x] - scale * (e[1, x + 1] - ey - (ex_yn - ex))
    h_out[0, x] = hx
    h_out[1, x] = hy
    h_out[2, x] = hz
    first_cols, last_cols = packs
    for group, v in enumerate((ex, ez, ey)):
        at = GAP * group + x
        first_cols = jnp.where(lane == at, pltpu.roll(v, at, 1), first_cols)
    for group, v in enumerate((hx, hz)):
        at = GAP * group + x
        last_cols = jnp.where(lane == at, pltpu.roll(v, at + 1, 1), last_cols)
    return first_cols, last_cols


def column_to_tile(column):
    row = jnp.sum(jnp.where(lanes() == rows(), column, 0.0), axis=0, keepdims=True)
    return jnp.broadcast_to(row, (8, YL))


def tile_to_column(tile):
    return jnp.sum(jnp.where(lanes() == rows(), tile[0:1], 0.0), axis=1, keepdims=True)


def h_full(x, hp, col_e, scale):
    last = lanes() == YL - 1
    ex_halo = pltpu.roll(col_e, YL - 1 - x, 1)
    ez_halo = pltpu.roll(col_e, YL - 1 - GAP - x, 1)
    hx = hp[0, x] - jnp.where(last, scale * ez_halo, 0.0)
    hz = hp[2, x] + jnp.where(last, scale * ex_halo, 0.0)
    return hx, hp[1, x], hz


def e_update(x, prev, hp, e, j, mat, col_e, col_h, decay, scale, outs):
    lane = lanes()
    e_out, h_out, j_out = outs
    hy_xp, hz_xp = prev
    first = lane == 0
    hx, hy, hz = h_full(x, hp, col_e, scale)
    h_out[0, x] = hx
    h_out[1, x] = hy
    h_out[2, x] = hz
    hx_yp = jnp.where(first, pltpu.roll(col_h, YL - x, 1), pltpu.roll(hx, 1, 1))
    hz_yp = jnp.where(first, pltpu.roll(col_h, YL - GAP - x, 1), pltpu.roll(hz, 1, 1))
    m = mat[x]
    metal = m == 2
    e_scale = scale * jnp.where(m == 1, 0.25, 1.0)
    backs = (
        hz - hz_yp - (hy - z_prev(hy)),
        hx - z_prev(hx) - (hz - hz_xp),
        hy - hy_xp - (hx - hx_yp),
    )
    for c, back in enumerate(backs):
        j_now = j[c, x]
        e_new = decay * e[c, x] + e_scale * (back - jnp.where(metal, j_now, 0.0))
        e_out[c, x] = e_new
        j_out[c, x] = jnp.where(metal, DRUDE_KEEP * j_now + DRUDE_GAIN * e_new, 0.0)
    return hy, hz


def slab_grad(z, e, col_e, w, level):
    nx = e.shape[1] - 1
    lane = lax.broadcasted_iota(jnp.int32, (nx, YL), 1)
    sub = lax.broadcasted_iota(jnp.int32, (nx, YL), 0)

    def cells(c, x, k):
        return e[c, pl.ds(x, nx), k]

    k = Z0 + z
    ex, ey, ez = cells(0, 0, k), cells(1, 0, k), cells(2, 0, k)
    ex_xn, ez_zn = cells(0, 1, k), cells(2, 0, k + 1)
    halo = jnp.sum(jnp.where(lane == 2 * GAP + sub, col_e[k : k + 1], 0.0), axis=1, keepdims=True)
    ey_yn = jnp.where(lane == YL - 1, halo, pltpu.roll(ey, YL - 1, 1))
    return 0.5 * (
        (ex + ex_xn) * w[level, 0, z] + (ey + ey_yn) * w[level, 1, z] + (ez + ez_zn) * w[level, 2, z]
    )


def exchange_kernel(
    gx, gy, nx,
    pml_in, tick_in, e_in, h_in, j_in, m_in, f_in,
    e1, h1, j1, e2, mat, w, grad, coef, rim_x, col_e_out, col_h_out,
    pml, tick, e0, hp, j0, fwd, pack_e, pack_h, send_h, tile_e, tile_h,
    got_e, got_slab, got_h, got_ye, got_yh, got_de, got_dh,
    field_sem, load_sem, send_sem, recv_sem,
):
    me_x = lax.axis_index("gx")
    me_y = lax.axis_index("gy")
    x_next, x_prev = lax.rem(me_x + 1, gx), lax.rem(me_x + gx - 1, gx)
    y_next, y_prev = lax.rem(me_y + 1, gy), lax.rem(me_y + gy - 1, gy)
    barrier = pltpu.get_barrier_semaphore()
    peers = (
        (x_prev, me_y), (x_next, me_y), (me_x, y_prev), (me_x, y_next), (x_next, y_prev), (x_prev, y_next),
    )
    for peer in peers:
        pl.semaphore_signal(barrier, inc=1, device_id=peer, device_id_type=MESH)

    small = [
        pltpu.make_async_copy(pml_in, pml, load_sem.at[3]),
        pltpu.make_async_copy(tick_in, tick, load_sem.at[4]),
    ]
    fields = []
    for i in reversed(range(CHUNKS)):
        span = pl.ds(i * nx // CHUNKS, nx // CHUNKS)
        fields.append(
            [
                pltpu.make_async_copy(e_in.at[:, span], e0.at[:, span], field_sem.at[0, i]),
                pltpu.make_async_copy(h_in.at[:, span], hp.at[:, span], field_sem.at[1, i]),
            ]
        )
    late = [
        pltpu.make_async_copy(f_in, fwd, load_sem.at[0]),
        pltpu.make_async_copy(j_in, j0, load_sem.at[1]),
        pltpu.make_async_copy(m_in, mat, load_sem.at[2]),
    ]
    for load in small + sum(fields, []) + late:
        load.start()
    for load in small:
        load.wait()

    lane = lanes()
    decay, scale = absorber(pml)
    coef[0] = decay
    coef[1] = scale
    zero = jnp.zeros((Z, YL), F32)
    for c in range(3):
        e0[c, nx] = zero
        e1[c, nx] = zero

    def route(level, i, e):
        src, dst, peer = (
            (e.at[pl.ds(1, 2), 0], got_e, 0),
            (e.at[0, 0, pl.ds(W0, WN)], got_slab, 0),
            (send_h.at[level], got_h, 1),
            (pack_e.at[level], got_ye, 2),
            (pack_h.at[level], got_yh, 3),
            (tile_e.at[level], got_de, 4),
            (tile_h.at[level], got_dh, 5),
        )[i]
        return pltpu.make_async_remote_copy(
            src_ref=src,
            dst_ref=dst.at[level],
            send_sem=send_sem.at[level, i],
            recv_sem=recv_sem.at[level, i],
            device_id=peers[peer],
            device_id_type=MESH,
        )

    def send(level, e, which):
        copies = [route(level, i, e) for i in which]
        for copy in copies:
            copy.start()
        return copies

    def pack(level, e, h, packs):
        pack_e[level] = packs[0]
        pack_h[level] = packs[1]
        send_h[level, 0] = h[1, nx - 1]
        send_h[level, 1] = h[2, nx - 1]
        tile_h[level] = column_to_tile(e[1, 0, :, YL - 1 : YL])
        tile_e[level] = column_to_tile(e[0, nx - 1, :, 0:1])

    def receive(level, e, h):
        e[0, nx, pl.ds(W0, WN)] = got_slab[level]
        h[1, nx - 1] = h[1, nx - 1] + scale * got_e[level, 1]
        h[2, nx - 1] = h[2, nx - 1] - scale * got_e[level, 0]
        own = pack_e[level]
        term = jnp.where(
            lane < GAP,
            -pltpu.roll(own, YL - GAP, 1),
            jnp.where(lane < 2 * GAP, pltpu.roll(own, GAP, 1), 0.0),
        )
        col_e_out[...] = got_ye[level]
        col_h_out[...] = got_yh[level] + scale * term

    def receive_corners(level, e):
        far = tile_to_column(got_dh[level])
        col_h_out[...] = col_h_out[...] - jnp.where(lane == GAP + nx - 1, scale * far, 0.0)
        corner = jnp.where(lane == YL - 1, tile_to_column(got_de[level]), 0.0)
        rim_x[0] = got_h[level, 0] + scale * e[2, 0]
        rim_x[1] = got_h[level, 1] + scale * (corner - e[1, 0])

    def plane(step, packs, e, h, h_out):
        return h_partial(nx - 2 - step, e, h, h_out, coef[0], coef[1], packs)

    packs = None
    for i, parts in enumerate(fields):
        for load in parts:
            load.wait()
        if i == 0:
            head = functools.partial(h_partial, nx - 1, e0, hp, hp, decay, scale)
            packs = head((zero, zero))
        size = nx // CHUNKS
        packs = lax.fori_loop(
            max(i * size - 1, 0),
            (i + 1) * size - 1,
            functools.partial(plane, e=e0, h=hp, h_out=hp),
            packs,
        )
    pack(0, e0, hp, packs)
    pl.semaphore_wait(barrier, len(peers))
    corners = send(0, e0, (5, 6))
    copies = send(0, e0, (4, 3, 2, 0, 1))

    late[0].wait()
    table = phase_table(tick)
    terms = [
        [jnp.broadcast_to(table[0:1, n * 8 + k : n * 8 + k + 1], (nx, YL)) for k in range(8)]
        for n in range(STEPS)
    ]

    def weigh(z, carry):
        for c in range(3):
            sums = [None, None]
            for k in range(8):
                value = fwd[k * 3 + c, z].astype(F32)
                for n in range(STEPS):
                    part = terms[n][k] * value
                    sums[n] = part if sums[n] is None else sums[n] + part
            for n in range(STEPS):
                w[n, c, z] = sums[n]
        return carry

    lax.fori_loop(0, DZ, weigh, 0)
    late[1].wait()
    late[2].wait()
    for copy in copies:
        copy.wait()

    receive(0, e0, hp)

    def advance(x, prev, e, h, j, e_next, j_next):
        return e_update(
            x, prev, h, e, j, mat, col_e_out[...], col_h_out[...], coef[0], coef[1], (e_next, h, j_next)
        )

    first = functools.partial(advance, e=e0, h=hp, j=j0, e_next=e1, j_next=j1)
    second = functools.partial(advance, e=e1, h=h1, j=j1, e_next=e2, j_next=j1)

    def inner(step, h):
        return lax.fori_loop(1, nx - 1, step, h_full(0, h, col_e_out[...], coef[1])[1:])

    prev = inner(first, hp)
    packs = lax.fori_loop(1, nx - 2, functools.partial(plane, e=e1, h=hp, h_out=h1), (zero, zero))
    for copy in corners:
        copy.wait()
    receive_corners(0, e0)
    first(0, (rim_x[0], rim_x[1]))
    copies = send(1, e1, (0, 1))
    first(nx - 1, prev)
    for x in (nx - 1, nx - 2, 0):
        packs = h_partial(x, e1, hp, h1, coef[0], coef[1], packs)
    pack(1, e1, h1, packs)
    corners = send(1, e1, (5, 6))
    copies += send(1, e1, (4, 3, 2))

    for z in range(DZ):
        grad[z] = slab_grad(z, e0, got_ye.at[0], w, 0)
    for copy in copies:
        copy.wait()
    receive(1, e1, h1)
    inner(second, h1)
    for copy in corners:
        copy.wait()
    receive_corners(1, e1)


def finish_kernel(
    nx,
    e1, h1, j1, e2, mat, w, grad, coef, rim_x, col_e, col_h,
    e_res, h_res, j_res, g_res,
    e_rim, h_rim, j_rim, g2, sem, g_sem,
):
    fields = ((e2, e_rim, e_res), (h1, h_rim, h_res), (j1, j_rim, j_res))
    mid = pl.ds(1, nx - 2)
    copies = [
        pltpu.make_async_copy(src.at[:, mid], dst.at[:, mid], sem.at[i, 0])
        for i, (src, _, dst) in enumerate(fields)
    ]
    for copy in copies:
        copy.start()
    last = nx - 1
    for n, x, prev in ((1, 0, (rim_x[0], rim_x[1])), (2, last, (h1[1, last - 1], h1[2, last - 1]))):
        e_update(
            x, prev, h1, e1, j1, mat, col_e[...], col_h[...], coef[0], coef[1], (e_rim, h_rim, j_rim)
        )
        for i, (_, src, dst) in enumerate(fields):
            copies.append(pltpu.make_async_copy(src.at[:, x], dst.at[:, x], sem.at[i, n]))
            copies[-1].start()
    for z in range(DZ):
        g2[z] = grad[z] + slab_grad(z, e1, col_e, w, 1)
    copies.append(pltpu.make_async_copy(g2, g_res, g_sem))
    copies[-1].start()
    for copy in copies:
        copy.wait()


def body(gx, gy, e_field, h_field, current, material, pml_cells, forward_field, time_index):
    nx = e_field.shape[1]
    slab = jnp.transpose(forward_field, (0, 2, 1, 3))
    field = (3, nx, Z, YL)
    padded = (3, nx + 1, Z, YL)
    plane = (Z, YL)
    any_spec = pl.BlockSpec(memory_space=pl.ANY)
    hbm = pl.BlockSpec(memory_space=pltpu.HBM)
    vmem = pl.BlockSpec(memory_space=pltpu.VMEM)
    kept = [
        (padded, F32), (field, F32), (field, F32), (field, F32), ((nx, Z, YL), jnp.int32), ((STEPS, 3, DZ, nx, YL), F32),
        ((DZ, nx, YL), F32), ((2,) + plane, F32), ((2,) + plane, F32), (plane, F32), (plane, F32),
    ]
    mid = pl.pallas_call(
        functools.partial(exchange_kernel, gx, gy, nx),
        out_shape=[pltpu.VMEM(shape, dtype) for shape, dtype in kept],
        in_specs=[hbm] * 7,
        out_specs=[vmem] * len(kept),
        scratch_shapes=[
            pltpu.SMEM((2,), jnp.int32),
            pltpu.SMEM((1,), jnp.int32),
            pltpu.VMEM(padded, F32),
            pltpu.VMEM(field, F32),
            pltpu.VMEM(field, F32),
            pltpu.VMEM(slab.shape, slab.dtype),
            pltpu.VMEM((STEPS,) + plane, F32),
            pltpu.VMEM((STEPS,) + plane, F32),
            pltpu.VMEM((STEPS, 2) + plane, F32),
            pltpu.VMEM((STEPS, 8, YL), F32),
            pltpu.VMEM((STEPS, 8, YL), F32),
            pltpu.VMEM((STEPS, 2) + plane, F32),
            pltpu.VMEM((STEPS, WN, YL), F32),
            pltpu.VMEM((STEPS, 2) + plane, F32),
            pltpu.VMEM((STEPS,) + plane, F32),
            pltpu.VMEM((STEPS,) + plane, F32),
            pltpu.VMEM((STEPS, 8, YL), F32),
            pltpu.VMEM((STEPS, 8, YL), F32),
            pltpu.SemaphoreType.DMA((2, CHUNKS)),
            pltpu.SemaphoreType.DMA((5,)),
            pltpu.SemaphoreType.DMA((STEPS, 7)),
            pltpu.SemaphoreType.DMA((STEPS, 7)),
        ],
        compiler_params=pltpu.CompilerParams(
            collective_id=0, has_side_effects=True, vmem_limit_bytes=57 << 20
        ),
        name="exchange",
    )(pml_cells, time_index, e_field, h_field, current, material, slab)
    e, h, j, grad = pl.pallas_call(
        functools.partial(finish_kernel, nx),
        out_shape=[
            jax.ShapeDtypeStruct(field, F32),
            jax.ShapeDtypeStruct(field, F32),
            jax.ShapeDtypeStruct(field, F32),
            jax.ShapeDtypeStruct((DZ, nx, YL), F32),
        ],
        in_specs=[vmem] * len(kept),
        out_specs=[any_spec] * 4,
        scratch_shapes=[
            pltpu.VMEM(field, F32),
            pltpu.VMEM(field, F32),
            pltpu.VMEM(field, F32),
            pltpu.VMEM((DZ, nx, YL), F32),
            pltpu.SemaphoreType.DMA((3, 3)),
            pltpu.SemaphoreType.DMA(()),
        ],
        compiler_params=pltpu.CompilerParams(vmem_limit_bytes=24 << 20),
        name="finish",
    )(*mid)
    return e, h, j, jnp.transpose(grad, (1, 0, 2))


def solution(mesh):
    field = P(None, "gx", None, "gy")
    cell = P("gx", None, "gy")
    return jax.shard_map(
        functools.partial(body, mesh.shape["gx"], mesh.shape["gy"]),
        mesh=mesh,
        in_specs=(field, field, field, cell, P(), field, P()),
        out_specs=(field, field, field, cell),
        check_vma=False,
    )
```

```python
import functools
import math

import jax
import jax.numpy as jnp
from jax import lax
from jax.experimental import pallas as pl
from jax.experimental.pallas import tpu as pltpu
from jax.sharding import PartitionSpec as P

Z = 48
DZ = 12
FREQ = 4
STEPS = 2
Z0 = 18
W0 = 16
WN = 16
YL = 128
CHUNKS = 4
GAP = 16

COURANT = 0.5
SIGMA_PEAK = 0.8
DRUDE_KEEP = 0.95 / 1.05
DRUDE_GAIN = 0.25 / 1.05
PERIOD_STEPS = 64
F32 = jnp.float32
MESH = pl.DeviceIdType.MESH


def lanes():
    return lax.broadcasted_iota(jnp.int32, (Z, YL), 1)


def rows():
    return lax.broadcasted_iota(jnp.int32, (Z, YL), 0)


def z_next(v):
    return jnp.where(rows() == Z - 1, 0.0, pltpu.roll(v, Z - 1, 0))


def z_prev(v):
    return jnp.where(rows() == 0, 0.0, pltpu.roll(v, 1, 0))


def absorber(pml):
    low = pml[0]
    high = pml[1]
    z = rows()
    low_depth = jnp.maximum(low - z, 0).astype(F32) / low.astype(F32)
    high_depth = jnp.maximum(z - (Z - 1 - high), 0).astype(F32) / high.astype(F32)
    sigma = SIGMA_PEAK * (low_depth * low_depth * low_depth + high_depth * high_depth * high_depth)
    half_loss = 1.0 + 0.5 * sigma
    return (1.0 - 0.5 * sigma) / half_loss, COURANT / half_loss


def phase_table(tick):
    lane = lax.broadcasted_iota(jnp.int32, (8, YL), 1)
    level = lane // 8
    freq = (lane % 8) // 2
    turn = ((3 + freq) * (tick[0] - level)) & (PERIOD_STEPS - 1)
    angle = turn.astype(F32) * (2.0 * math.pi / PERIOD_STEPS)
    return jnp.where(lane % 2 == 0, jnp.cos(angle), -jnp.sin(angle))


def h_partial(x, e, h, h_out, decay, scale, packs):
    lane = lanes()
    ex, ey, ez = e[0, x], e[1, x], e[2, x]
    last = lane == YL - 1
    ez_yn = jnp.where(last, 0.0, pltpu.roll(ez, YL - 1, 1))
    ex_yn = jnp.where(last, 0.0, pltpu.roll(ex, YL - 1, 1))
    hx = decay * h[0, x] - scale * (ez_yn - ez - (z_next(ey) - ey))
    hy = decay * h[1, x] - scale * (z_next(ex) - ex - (e[2, x + 1] - ez))
    hz = decay * h[2, x] - scale * (e[1, x + 1] - ey - (ex_yn - ex))
    h_out[0, x] = hx
    h_out[1, x] = hy
    h_out[2, x] = hz
    first_cols, last_cols = packs
    for group, v in enumerate((ex, ez, ey)):
        at = GAP * group + x
        first_cols = jnp.where(lane == at, pltpu.roll(v, at, 1), first_cols)
    for group, v in enumerate((hx, hz)):
        at = GAP * group + x
        last_cols = jnp.where(lane == at, pltpu.roll(v, at + 1, 1), last_cols)
    return first_cols, last_cols


def column_to_tile(column):
    row = jnp.sum(jnp.where(lanes() == rows(), column, 0.0), axis=0, keepdims=True)
    return jnp.broadcast_to(row, (8, YL))


def tile_to_column(tile):
    return jnp.sum(jnp.where(lanes() == rows(), tile[0:1], 0.0), axis=1, keepdims=True)


def h_full(x, hp, col_e, scale):
    last = lanes() == YL - 1
    ex_halo = pltpu.roll(col_e, YL - 1 - x, 1)
    ez_halo = pltpu.roll(col_e, YL - 1 - GAP - x, 1)
    hx = hp[0, x] - jnp.where(last, scale * ez_halo, 0.0)
    hz = hp[2, x] + jnp.where(last, scale * ex_halo, 0.0)
    return hx, hp[1, x], hz


def e_update(x, prev, hp, e, j, mats, col_e, col_h, decay, scale, outs):
    lane = lanes()
    e_out, h_out, j_out = outs
    hy_xp, hz_xp = prev
    first = lane == 0
    hx, hy, hz = h_full(x, hp, col_e, scale)
    h_out[0, x] = hx
    h_out[1, x] = hy
    h_out[2, x] = hz
    hx_yp = jnp.where(first, pltpu.roll(col_h, YL - x, 1), pltpu.roll(hx, 1, 1))
    hz_yp = jnp.where(first, pltpu.roll(col_h, YL - GAP - x, 1), pltpu.roll(hz, 1, 1))
    e_scale, gain = mats[0, x], mats[1, x]
    backs = (
        hz - hz_yp - (hy - z_prev(hy)),
        hx - z_prev(hx) - (hz - hz_xp),
        hy - hy_xp - (hx - hx_yp),
    )
    for c, back in enumerate(backs):
        j_now = j[c, x]
        e_new = decay * e[c, x] + e_scale * (back - j_now)
        e_out[c, x] = e_new
        j_out[c, x] = DRUDE_KEEP * j_now + gain * e_new
    return hy, hz


def slab_grad(z, e, col_e, w, level):
    nx = e.shape[1] - 1
    lane = lax.broadcasted_iota(jnp.int32, (nx, YL), 1)
    sub = lax.broadcasted_iota(jnp.int32, (nx, YL), 0)

    def cells(c, x, k):
        return e[c, pl.ds(x, nx), k]

    k = Z0 + z
    ex, ey, ez = cells(0, 0, k), cells(1, 0, k), cells(2, 0, k)
    ex_xn, ez_zn = cells(0, 1, k), cells(2, 0, k + 1)
    halo = jnp.sum(jnp.where(lane == 2 * GAP + sub, col_e[k : k + 1], 0.0), axis=1, keepdims=True)
    ey_yn = jnp.where(lane == YL - 1, halo, pltpu.roll(ey, YL - 1, 1))
    return 0.5 * (
        (ex + ex_xn) * w[level, 0, z] + (ey + ey_yn) * w[level, 1, z] + (ez + ez_zn) * w[level, 2, z]
    )


def exchange_kernel(
    gx, gy, nx,
    pml_in, tick_in, e_in, h_in, j_in, m_in, f_in,
    e1, h1, j1, mats, w, grad, coef, rim_x, col_e_out, col_h_out,
    pml, tick, e0, hp, j0, mat, fwd, pack_e, pack_h, send_h, tile_e, tile_h,
    got_e, got_slab, got_h, got_ye, got_yh, got_de, got_dh,
    field_sem, load_sem, send_sem, recv_sem,
):
    me_x = lax.axis_index("gx")
    me_y = lax.axis_index("gy")
    x_next, x_prev = lax.rem(me_x + 1, gx), lax.rem(me_x + gx - 1, gx)
    y_next, y_prev = lax.rem(me_y + 1, gy), lax.rem(me_y + gy - 1, gy)
    barrier = pltpu.get_barrier_semaphore()
    peers = (
        (x_prev, me_y), (x_next, me_y), (me_x, y_prev), (me_x, y_next), (x_next, y_prev), (x_prev, y_next),
    )
    for peer in peers:
        pl.semaphore_signal(barrier, inc=1, device_id=peer, device_id_type=MESH)

    small = [
        pltpu.make_async_copy(pml_in, pml, load_sem.at[3]),
        pltpu.make_async_copy(tick_in, tick, load_sem.at[4]),
    ]
    fields = []
    for i in reversed(range(CHUNKS)):
        span = pl.ds(i * nx // CHUNKS, nx // CHUNKS)
        fields.append(
            [
                pltpu.make_async_copy(e_in.at[:, span], e0.at[:, span], field_sem.at[0, i]),
                pltpu.make_async_copy(h_in.at[:, span], hp.at[:, span], field_sem.at[1, i]),
            ]
        )
    late = [
        pltpu.make_async_copy(f_in, fwd, load_sem.at[0]),
        pltpu.make_async_copy(j_in, j0, load_sem.at[1]),
        pltpu.make_async_copy(m_in, mat, load_sem.at[2]),
    ]
    for load in small + sum(fields, []) + late:
        load.start()
    for load in small:
        load.wait()

    lane = lanes()
    decay, scale = absorber(pml)
    coef[0] = decay
    coef[1] = scale
    zero = jnp.zeros((Z, YL), F32)
    for c in range(3):
        e0[c, nx] = zero
        e1[c, nx] = zero

    def route(level, i, e):
        src, dst, peer = (
            (e.at[pl.ds(1, 2), 0], got_e, 0),
            (e.at[0, 0, pl.ds(W0, WN)], got_slab, 0),
            (send_h.at[level], got_h, 1),
            (pack_e.at[level], got_ye, 2),
            (pack_h.at[level], got_yh, 3),
            (tile_e.at[level], got_de, 4),
            (tile_h.at[level], got_dh, 5),
        )[i]
        return pltpu.make_async_remote_copy(
            src_ref=src,
            dst_ref=dst.at[level],
            send_sem=send_sem.at[level, i],
            recv_sem=recv_sem.at[level, i],
            device_id=peers[peer],
            device_id_type=MESH,
        )

    def send(level, e, which):
        copies = [route(level, i, e) for i in which]
        for copy in copies:
            copy.start()
        return copies

    def pack(level, packs):
        pack_e[level] = packs[0]
        pack_h[level] = packs[1]

    def rim(level, e, h):
        send_h[level, 0] = h[1, nx - 1]
        send_h[level, 1] = h[2, nx - 1]
        tile_h[level] = column_to_tile(e[1, 0, :, YL - 1 : YL])
        tile_e[level] = column_to_tile(e[0, nx - 1, :, 0:1])

    def receive(level, e, h):
        e[0, nx, pl.ds(W0, WN)] = got_slab[level]
        h[1, nx - 1] = h[1, nx - 1] + scale * got_e[level, 1]
        h[2, nx - 1] = h[2, nx - 1] - scale * got_e[level, 0]
        corner = jnp.where(lane == YL - 1, tile_to_column(got_de[level]), 0.0)
        hy = got_h[level, 0] + scale * e[2, 0]
        hz = got_h[level, 1] + scale * (corner - e[1, 0])
        own = pack_e[level]
        term = jnp.where(
            lane < GAP,
            -pltpu.roll(own, YL - GAP, 1),
            jnp.where(lane < 2 * GAP, pltpu.roll(own, GAP, 1), 0.0),
        )
        term = term - jnp.where(lane == GAP + nx - 1, tile_to_column(got_dh[level]), 0.0)
        return hy, hz, got_ye[level], got_yh[level] + scale * term

    def plane(step, packs, e, h, h_out):
        return h_partial(nx - 2 - step, e, h, h_out, coef[0], coef[1], packs)

    packs = None
    for i, parts in enumerate(fields):
        for load in parts:
            load.wait()
        if i == 0:
            head = functools.partial(h_partial, nx - 1, e0, hp, hp, decay, scale)
            packs = head((zero, zero))
        size = nx // CHUNKS
        packs = lax.fori_loop(
            max(i * size - 1, 0),
            (i + 1) * size - 1,
            functools.partial(plane, e=e0, h=hp, h_out=hp),
            packs,
        )
    pack(0, packs)
    rim(0, e0, hp)
    pl.semaphore_wait(barrier, len(peers))
    copies = send(0, e0, (5, 4, 3, 2, 0, 1, 6))

    late[0].wait()
    table = phase_table(tick)
    terms = [
        [jnp.broadcast_to(table[0:1, n * 8 + k : n * 8 + k + 1], (nx, YL)) for k in range(8)]
        for n in range(STEPS)
    ]

    def weigh(z, carry):
        for c in range(3):
            sums = [None, None]
            for k in range(8):
                value = fwd[k * 3 + c, z].astype(F32)
                for n in range(STEPS):
                    part = terms[n][k] * value
                    sums[n] = part if sums[n] is None else sums[n] + part
            for n in range(STEPS):
                w[n, c, z] = sums[n]
        return carry

    lax.fori_loop(0, DZ, weigh, 0)
    late[1].wait()
    late[2].wait()

    def materials(x, carry):
        m = mat[x]
        metal = m == 2
        mats[0, x] = coef[1] * jnp.where(m == 1, 0.25, 1.0)
        mats[1, x] = jnp.where(metal, DRUDE_GAIN, 0.0)
        for c in range(3):
            j0[c, x] = jnp.where(metal, j0[c, x], 0.0)
        return carry

    lax.fori_loop(0, nx, materials, 0)
    for copy in copies:
        copy.wait()

    hy, hz, col_e, col_h = receive(0, e0, hp)
    col_e_out[...] = col_e
    col_h_out[...] = col_h

    def advance(x, prev):
        return e_update(
            x, prev, hp, e0, j0, mats, col_e_out[...], col_h_out[...], coef[0], coef[1], (e1, hp, j1)
        )

    prev = advance(0, (hy, hz))
    copies = send(1, e1, (0, 1))
    advance(nx - 1, h_full(nx - 2, hp, col_e_out[...], coef[1])[1:])
    pack(1, h_partial(nx - 1, e1, hp, h1, coef[0], coef[1], (zero, zero)))
    rim(1, e1, h1)
    copies += send(1, e1, (2, 5, 6))
    lax.fori_loop(1, nx - 1, advance, prev)
    packs = (pack_e[1], pack_h[1])
    pack(1, lax.fori_loop(0, nx - 1, functools.partial(plane, e=e1, h=hp, h_out=h1), packs))
    copies += send(1, e1, (3, 4))

    for z in range(DZ):
        grad[z] = slab_grad(z, e0, got_ye.at[0], w, 0)
    for copy in copies:
        copy.wait()
    hy, hz, col_e, col_h = receive(1, e1, h1)
    rim_x[0] = hy
    rim_x[1] = hz
    col_e_out[...] = col_e
    col_h_out[...] = col_h


def finish_kernel(
    nx,
    e1, h1, j1, mats, w, grad, coef, rim_x, col_e, col_h,
    e_res, h_res, j_res, g_res,
    e2, h2, j2, g2, sem, g_sem,
):
    def copies(x):
        return [
            pltpu.make_async_copy(src.at[:, x], dst.at[:, x], sem.at[i, x])
            for i, (src, dst) in enumerate(((e2, e_res), (h2, h_res), (j2, j_res)))
        ]

    def advance(x, prev):
        out = e_update(
            x, prev, h1, e1, j1, mats, col_e[...], col_h[...], coef[0], coef[1], (e2, h2, j2)
        )
        for copy in copies(x):
            copy.start()
        return out

    lax.fori_loop(0, nx, advance, (rim_x[0], rim_x[1]))
    for z in range(DZ):
        g2[z] = grad[z] + slab_grad(z, e1, col_e, w, 1)
    g_copy = pltpu.make_async_copy(g2, g_res, g_sem)
    g_copy.start()

    def drain(x, carry):
        for copy in copies(x):
            copy.wait()
        return carry

    lax.fori_loop(0, nx, drain, 0)
    g_copy.wait()


def body(gx, gy, e_field, h_field, current, material, pml_cells, forward_field, time_index):
    nx = e_field.shape[1]
    slab = jnp.transpose(forward_field, (0, 2, 1, 3))
    field = (3, nx, Z, YL)
    padded = (3, nx + 1, Z, YL)
    plane = (Z, YL)
    any_spec = pl.BlockSpec(memory_space=pl.ANY)
    hbm = pl.BlockSpec(memory_space=pltpu.HBM)
    vmem = pl.BlockSpec(memory_space=pltpu.VMEM)
    kept = [
        (padded, F32), (field, F32), (field, F32), ((2, nx, Z, YL), F32), ((STEPS, 3, DZ, nx, YL), F32),
        ((DZ, nx, YL), F32), ((2,) + plane, F32), ((2,) + plane, F32), (plane, F32), (plane, F32),
    ]
    mid = pl.pallas_call(
        functools.partial(exchange_kernel, gx, gy, nx),
        out_shape=[pltpu.VMEM(shape, dtype) for shape, dtype in kept],
        in_specs=[hbm] * 7,
        out_specs=[vmem] * len(kept),
        scratch_shapes=[
            pltpu.SMEM((2,), jnp.int32),
            pltpu.SMEM((1,), jnp.int32),
            pltpu.VMEM(padded, F32),
            pltpu.VMEM(field, F32),
            pltpu.VMEM(field, F32),
            pltpu.VMEM((nx, Z, YL), jnp.int32),
            pltpu.VMEM(slab.shape, slab.dtype),
            pltpu.VMEM((STEPS,) + plane, F32),
            pltpu.VMEM((STEPS,) + plane, F32),
            pltpu.VMEM((STEPS, 2) + plane, F32),
            pltpu.VMEM((STEPS, 8, YL), F32),
            pltpu.VMEM((STEPS, 8, YL), F32),
            pltpu.VMEM((STEPS, 2) + plane, F32),
            pltpu.VMEM((STEPS, WN, YL), F32),
            pltpu.VMEM((STEPS, 2) + plane, F32),
            pltpu.VMEM((STEPS,) + plane, F32),
            pltpu.VMEM((STEPS,) + plane, F32),
            pltpu.VMEM((STEPS, 8, YL), F32),
            pltpu.VMEM((STEPS, 8, YL), F32),
            pltpu.SemaphoreType.DMA((2, CHUNKS)),
            pltpu.SemaphoreType.DMA((5,)),
            pltpu.SemaphoreType.DMA((STEPS, 7)),
            pltpu.SemaphoreType.DMA((STEPS, 7)),
        ],
        compiler_params=pltpu.CompilerParams(
            collective_id=0, has_side_effects=True, vmem_limit_bytes=57 << 20
        ),
        name="exchange",
    )(pml_cells, time_index, e_field, h_field, current, material, slab)
    e, h, j, grad = pl.pallas_call(
        functools.partial(finish_kernel, nx),
        out_shape=[
            jax.ShapeDtypeStruct(field, F32),
            jax.ShapeDtypeStruct(field, F32),
            jax.ShapeDtypeStruct(field, F32),
            jax.ShapeDtypeStruct((DZ, nx, YL), F32),
        ],
        in_specs=[vmem] * len(kept),
        out_specs=[any_spec] * 4,
        scratch_shapes=[
            pltpu.VMEM(field, F32),
            pltpu.VMEM(field, F32),
            pltpu.VMEM(field, F32),
            pltpu.VMEM((DZ, nx, YL), F32),
            pltpu.SemaphoreType.DMA((3, nx)),
            pltpu.SemaphoreType.DMA(()),
        ],
        compiler_params=pltpu.CompilerParams(vmem_limit_bytes=24 << 20),
        name="finish",
    )(*mid)
    return e, h, j, jnp.transpose(grad, (1, 0, 2))


def solution(mesh):
    field = P(None, "gx", None, "gy")
    cell = P("gx", None, "gy")
    return jax.shard_map(
        functools.partial(body, mesh.shape["gx"], mesh.shape["gy"]),
        mesh=mesh,
        in_specs=(field, field, field, cell, P(), field, P()),
        out_specs=(field, field, field, cell),
        check_vma=False,
    )
```

```python
import functools
import math

import jax
import jax.numpy as jnp
from jax import lax
from jax.experimental import pallas as pl
from jax.experimental.pallas import tpu as pltpu
from jax.sharding import PartitionSpec as P

Z = 48
DZ = 12
FREQ = 4
STEPS = 2
Z0 = 18
W0 = 16
WN = 16
YL = 128
CHUNKS = 4
GAP = 16

COURANT = 0.5
SIGMA_PEAK = 0.8
DRUDE_KEEP = 0.95 / 1.05
DRUDE_GAIN = 0.25 / 1.05
PERIOD_STEPS = 64
F32 = jnp.float32
MESH = pl.DeviceIdType.MESH


def lanes():
    return lax.broadcasted_iota(jnp.int32, (Z, YL), 1)


def rows():
    return lax.broadcasted_iota(jnp.int32, (Z, YL), 0)


def z_next(v):
    return jnp.where(rows() == Z - 1, 0.0, pltpu.roll(v, Z - 1, 0))


def z_prev(v):
    return jnp.where(rows() == 0, 0.0, pltpu.roll(v, 1, 0))


def absorber(pml):
    low = pml[0]
    high = pml[1]
    z = rows()
    low_depth = jnp.maximum(low - z, 0).astype(F32) / low.astype(F32)
    high_depth = jnp.maximum(z - (Z - 1 - high), 0).astype(F32) / high.astype(F32)
    sigma = SIGMA_PEAK * (low_depth * low_depth * low_depth + high_depth * high_depth * high_depth)
    half_loss = 1.0 + 0.5 * sigma
    return (1.0 - 0.5 * sigma) / half_loss, COURANT / half_loss


def phase_table(tick):
    lane = lax.broadcasted_iota(jnp.int32, (8, YL), 1)
    level = lane // 8
    freq = (lane % 8) // 2
    turn = ((3 + freq) * (tick[0] - level)) & (PERIOD_STEPS - 1)
    angle = turn.astype(F32) * (2.0 * math.pi / PERIOD_STEPS)
    return jnp.where(lane % 2 == 0, jnp.cos(angle), -jnp.sin(angle))


def h_partial(x, e, h, h_out, decay, scale, packs):
    lane = lanes()
    ex, ey, ez = e[0, x], e[1, x], e[2, x]
    last = lane == YL - 1
    ez_yn = jnp.where(last, 0.0, pltpu.roll(ez, YL - 1, 1))
    ex_yn = jnp.where(last, 0.0, pltpu.roll(ex, YL - 1, 1))
    hx = decay * h[0, x] - scale * (ez_yn - ez - (z_next(ey) - ey))
    hy = decay * h[1, x] - scale * (z_next(ex) - ex - (e[2, x + 1] - ez))
    hz = decay * h[2, x] - scale * (e[1, x + 1] - ey - (ex_yn - ex))
    h_out[0, x] = hx
    h_out[1, x] = hy
    h_out[2, x] = hz
    first_cols, last_cols = packs
    for group, v in enumerate((ex, ez, ey)):
        at = GAP * group + x
        first_cols = jnp.where(lane == at, pltpu.roll(v, at, 1), first_cols)
    for group, v in enumerate((hx, hz)):
        at = GAP * group + x
        last_cols = jnp.where(lane == at, pltpu.roll(v, at + 1, 1), last_cols)
    return first_cols, last_cols


def column_to_tile(column):
    row = jnp.sum(jnp.where(lanes() == rows(), column, 0.0), axis=0, keepdims=True)
    return jnp.broadcast_to(row, (8, YL))


def tile_to_column(tile):
    return jnp.sum(jnp.where(lanes() == rows(), tile[0:1], 0.0), axis=1, keepdims=True)


def h_full(x, hp, col_e, scale):
    last = lanes() == YL - 1
    ex_halo = pltpu.roll(col_e, YL - 1 - x, 1)
    ez_halo = pltpu.roll(col_e, YL - 1 - GAP - x, 1)
    hx = hp[0, x] - jnp.where(last, scale * ez_halo, 0.0)
    hz = hp[2, x] + jnp.where(last, scale * ex_halo, 0.0)
    return hx, hp[1, x], hz


def e_update(x, prev, hp, e, j, mats, col_e, col_h, decay, scale, outs):
    lane = lanes()
    e_out, h_out, j_out = outs
    hy_xp, hz_xp = prev
    first = lane == 0
    hx, hy, hz = h_full(x, hp, col_e, scale)
    h_out[0, x] = hx
    h_out[1, x] = hy
    h_out[2, x] = hz
    hx_yp = jnp.where(first, pltpu.roll(col_h, YL - x, 1), pltpu.roll(hx, 1, 1))
    hz_yp = jnp.where(first, pltpu.roll(col_h, YL - GAP - x, 1), pltpu.roll(hz, 1, 1))
    e_scale, gain = mats[0, x], mats[1, x]
    backs = (
        hz - hz_yp - (hy - z_prev(hy)),
        hx - z_prev(hx) - (hz - hz_xp),
        hy - hy_xp - (hx - hx_yp),
    )
    for c, back in enumerate(backs):
        j_now = j[c, x]
        e_new = decay * e[c, x] + e_scale * (back - j_now)
        e_out[c, x] = e_new
        j_out[c, x] = DRUDE_KEEP * j_now + gain * e_new
    return hy, hz


def slab_grad(z, e, col_e, w, level):
    nx = e.shape[1] - 1
    lane = lax.broadcasted_iota(jnp.int32, (nx, YL), 1)
    sub = lax.broadcasted_iota(jnp.int32, (nx, YL), 0)

    def cells(c, x, k):
        return e[c, pl.ds(x, nx), k]

    k = Z0 + z
    ex, ey, ez = cells(0, 0, k), cells(1, 0, k), cells(2, 0, k)
    ex_xn, ez_zn = cells(0, 1, k), cells(2, 0, k + 1)
    halo = jnp.sum(jnp.where(lane == 2 * GAP + sub, col_e[k : k + 1], 0.0), axis=1, keepdims=True)
    ey_yn = jnp.where(lane == YL - 1, halo, pltpu.roll(ey, YL - 1, 1))
    return 0.5 * (
        (ex + ex_xn) * w[level, 0, z] + (ey + ey_yn) * w[level, 1, z] + (ez + ez_zn) * w[level, 2, z]
    )


def exchange_kernel(
    gx, gy, nx,
    pml_in, tick_in, e_in, h_in, j_in, m_in, f_in,
    e1, h1, j1, mats, w, grad, coef, rim_x, col_e_out, col_h_out,
    pml, tick, e0, hp, j0, mat, fwd, pack_e, pack_h, send_h, tile_e, tile_h,
    got_e, got_slab, got_h, got_ye, got_yh, got_de, got_dh,
    field_sem, load_sem, send_sem, recv_sem,
):
    me_x = lax.axis_index("gx")
    me_y = lax.axis_index("gy")
    x_next, x_prev = lax.rem(me_x + 1, gx), lax.rem(me_x + gx - 1, gx)
    y_next, y_prev = lax.rem(me_y + 1, gy), lax.rem(me_y + gy - 1, gy)
    barrier = pltpu.get_barrier_semaphore()
    peers = (
        (x_prev, me_y), (x_next, me_y), (me_x, y_prev), (me_x, y_next), (x_next, y_prev), (x_prev, y_next),
    )
    for peer in peers:
        pl.semaphore_signal(barrier, inc=1, device_id=peer, device_id_type=MESH)

    small = [
        pltpu.make_async_copy(pml_in, pml, load_sem.at[3]),
        pltpu.make_async_copy(tick_in, tick, load_sem.at[4]),
    ]
    fields = []
    for i in reversed(range(CHUNKS)):
        span = pl.ds(i * nx // CHUNKS, nx // CHUNKS)
        fields.append(
            [
                pltpu.make_async_copy(e_in.at[:, span], e0.at[:, span], field_sem.at[0, i]),
                pltpu.make_async_copy(h_in.at[:, span], hp.at[:, span], field_sem.at[1, i]),
            ]
        )
    late = [
        pltpu.make_async_copy(f_in, fwd, load_sem.at[0]),
        pltpu.make_async_copy(j_in, j0, load_sem.at[1]),
        pltpu.make_async_copy(m_in, mat, load_sem.at[2]),
    ]
    for load in small + sum(fields, []) + late:
        load.start()
    for load in small:
        load.wait()

    lane = lanes()
    decay, scale = absorber(pml)
    coef[0] = decay
    coef[1] = scale
    zero = jnp.zeros((Z, YL), F32)
    for c in range(3):
        e0[c, nx] = zero
        e1[c, nx] = zero

    def route(level, i, e):
        src, dst, peer = (
            (e.at[pl.ds(1, 2), 0], got_e, 0),
            (e.at[0, 0, pl.ds(W0, WN)], got_slab, 0),
            (send_h.at[level], got_h, 1),
            (pack_e.at[level], got_ye, 2),
            (pack_h.at[level], got_yh, 3),
            (tile_e.at[level], got_de, 4),
            (tile_h.at[level], got_dh, 5),
        )[i]
        return pltpu.make_async_remote_copy(
            src_ref=src,
            dst_ref=dst.at[level],
            send_sem=send_sem.at[level, i],
            recv_sem=recv_sem.at[level, i],
            device_id=peers[peer],
            device_id_type=MESH,
        )

    def send(level, e, which):
        copies = [route(level, i, e) for i in which]
        for copy in copies:
            copy.start()
        return copies

    def pack(level, packs):
        pack_e[level] = packs[0]
        pack_h[level] = packs[1]

    def rim(level, e, h):
        send_h[level, 0] = h[1, nx - 1]
        send_h[level, 1] = h[2, nx - 1]
        tile_h[level] = column_to_tile(e[1, 0, :, YL - 1 : YL])
        tile_e[level] = column_to_tile(e[0, nx - 1, :, 0:1])

    def receive(level, e, h):
        e[0, nx, pl.ds(W0, WN)] = got_slab[level]
        h[1, nx - 1] = h[1, nx - 1] + scale * got_e[level, 1]
        h[2, nx - 1] = h[2, nx - 1] - scale * got_e[level, 0]
        corner = jnp.where(lane == YL - 1, tile_to_column(got_de[level]), 0.0)
        hy = got_h[level, 0] + scale * e[2, 0]
        hz = got_h[level, 1] + scale * (corner - e[1, 0])
        own = pack_e[level]
        term = jnp.where(
            lane < GAP,
            -pltpu.roll(own, YL - GAP, 1),
            jnp.where(lane < 2 * GAP, pltpu.roll(own, GAP, 1), 0.0),
        )
        term = term - jnp.where(lane == GAP + nx - 1, tile_to_column(got_dh[level]), 0.0)
        return hy, hz, got_ye[level], got_yh[level] + scale * term

    def plane(step, packs, e, h, h_out):
        return h_partial(nx - 2 - step, e, h, h_out, coef[0], coef[1], packs)

    packs = None
    for i, parts in enumerate(fields):
        for load in parts:
            load.wait()
        if i == 0:
            head = functools.partial(h_partial, nx - 1, e0, hp, hp, decay, scale)
            packs = head((zero, zero))
        size = nx // CHUNKS
        packs = lax.fori_loop(
            max(i * size - 1, 0),
            (i + 1) * size - 1,
            functools.partial(plane, e=e0, h=hp, h_out=hp),
            packs,
        )
    pack(0, packs)
    rim(0, e0, hp)
    pl.semaphore_wait(barrier, len(peers))
    copies = send(0, e0, (5, 4, 3, 2, 0, 1, 6))

    late[0].wait()
    table = phase_table(tick)
    terms = [
        [jnp.broadcast_to(table[0:1, n * 8 + k : n * 8 + k + 1], (nx, YL)) for k in range(8)]
        for n in range(STEPS)
    ]

    def weigh(z, carry):
        for c in range(3):
            sums = [None, None]
            for k in range(8):
                value = fwd[k * 3 + c, z].astype(F32)
                for n in range(STEPS):
                    part = terms[n][k] * value
                    sums[n] = part if sums[n] is None else sums[n] + part
            for n in range(STEPS):
                w[n, c, z] = sums[n]
        return carry

    lax.fori_loop(0, DZ, weigh, 0)
    late[1].wait()
    late[2].wait()

    def materials(x, carry):
        m = mat[x]
        metal = m == 2
        mats[0, x] = coef[1] * jnp.where(m == 1, 0.25, 1.0)
        mats[1, x] = jnp.where(metal, DRUDE_GAIN, 0.0)
        for c in range(3):
            j0[c, x] = jnp.where(metal, j0[c, x], 0.0)
        return carry

    lax.fori_loop(0, nx, materials, 0)
    for copy in copies:
        copy.wait()

    hy, hz, col_e, col_h = receive(0, e0, hp)
    col_e_out[...] = col_e
    col_h_out[...] = col_h

    def advance(x, prev):
        return e_update(
            x, prev, hp, e0, j0, mats, col_e_out[...], col_h_out[...], coef[0], coef[1], (e1, hp, j1)
        )

    prev = advance(0, (hy, hz))
    copies = send(1, e1, (0, 1))
    advance(nx - 1, h_full(nx - 2, hp, col_e_out[...], coef[1])[1:])
    pack(1, h_partial(nx - 1, e1, hp, h1, coef[0], coef[1], (zero, zero)))
    rim(1, e1, h1)
    copies += send(1, e1, (2, 5, 6))
    lax.fori_loop(1, nx - 1, advance, prev)
    packs = (pack_e[1], pack_h[1])
    pack(1, lax.fori_loop(0, nx - 1, functools.partial(plane, e=e1, h=hp, h_out=h1), packs))
    copies += send(1, e1, (3, 4))

    for z in range(DZ):
        grad[z] = slab_grad(z, e0, got_ye.at[0], w, 0)
    for copy in copies:
        copy.wait()
    hy, hz, col_e, col_h = receive(1, e1, h1)
    rim_x[0] = hy
    rim_x[1] = hz
    col_e_out[...] = col_e
    col_h_out[...] = col_h


def finish_kernel(
    nx,
    e1, h1, j1, mats, w, grad, coef, rim_x, col_e, col_h,
    e_res, h_res, j_res, g_res,
    e2, h2, j2, g2, sem, g_sem,
):
    size = nx // CHUNKS
    copies = []

    def advance(x, prev):
        return e_update(
            x, prev, h1, e1, j1, mats, col_e[...], col_h[...], coef[0], coef[1], (e2, h2, j2)
        )

    prev = (rim_x[0], rim_x[1])
    for n in range(CHUNKS):
        prev = lax.fori_loop(n * size, (n + 1) * size, advance, prev)
        span = pl.ds(n * size, size)
        for i, (src, dst) in enumerate(((e2, e_res), (h2, h_res), (j2, j_res))):
            copies.append(pltpu.make_async_copy(src.at[:, span], dst.at[:, span], sem.at[i, n]))
            copies[-1].start()
    for z in range(DZ):
        g2[z] = grad[z] + slab_grad(z, e1, col_e, w, 1)
    copies.append(pltpu.make_async_copy(g2, g_res, g_sem))
    copies[-1].start()
    for copy in copies:
        copy.wait()


def body(gx, gy, e_field, h_field, current, material, pml_cells, forward_field, time_index):
    nx = e_field.shape[1]
    slab = jnp.transpose(forward_field, (0, 2, 1, 3))
    field = (3, nx, Z, YL)
    padded = (3, nx + 1, Z, YL)
    plane = (Z, YL)
    any_spec = pl.BlockSpec(memory_space=pl.ANY)
    hbm = pl.BlockSpec(memory_space=pltpu.HBM)
    vmem = pl.BlockSpec(memory_space=pltpu.VMEM)
    kept = [
        (padded, F32), (field, F32), (field, F32), ((2, nx, Z, YL), F32), ((STEPS, 3, DZ, nx, YL), F32),
        ((DZ, nx, YL), F32), ((2,) + plane, F32), ((2,) + plane, F32), (plane, F32), (plane, F32),
    ]
    mid = pl.pallas_call(
        functools.partial(exchange_kernel, gx, gy, nx),
        out_shape=[pltpu.VMEM(shape, dtype) for shape, dtype in kept],
        in_specs=[hbm] * 7,
        out_specs=[vmem] * len(kept),
        scratch_shapes=[
            pltpu.SMEM((2,), jnp.int32),
            pltpu.SMEM((1,), jnp.int32),
            pltpu.VMEM(padded, F32),
            pltpu.VMEM(field, F32),
            pltpu.VMEM(field, F32),
            pltpu.VMEM((nx, Z, YL), jnp.int32),
            pltpu.VMEM(slab.shape, slab.dtype),
            pltpu.VMEM((STEPS,) + plane, F32),
            pltpu.VMEM((STEPS,) + plane, F32),
            pltpu.VMEM((STEPS, 2) + plane, F32),
            pltpu.VMEM((STEPS, 8, YL), F32),
            pltpu.VMEM((STEPS, 8, YL), F32),
            pltpu.VMEM((STEPS, 2) + plane, F32),
            pltpu.VMEM((STEPS, WN, YL), F32),
            pltpu.VMEM((STEPS, 2) + plane, F32),
            pltpu.VMEM((STEPS,) + plane, F32),
            pltpu.VMEM((STEPS,) + plane, F32),
            pltpu.VMEM((STEPS, 8, YL), F32),
            pltpu.VMEM((STEPS, 8, YL), F32),
            pltpu.SemaphoreType.DMA((2, CHUNKS)),
            pltpu.SemaphoreType.DMA((5,)),
            pltpu.SemaphoreType.DMA((STEPS, 7)),
            pltpu.SemaphoreType.DMA((STEPS, 7)),
        ],
        compiler_params=pltpu.CompilerParams(
            collective_id=0, has_side_effects=True, vmem_limit_bytes=57 << 20
        ),
        name="exchange",
    )(pml_cells, time_index, e_field, h_field, current, material, slab)
    e, h, j, grad = pl.pallas_call(
        functools.partial(finish_kernel, nx),
        out_shape=[
            jax.ShapeDtypeStruct(field, F32),
            jax.ShapeDtypeStruct(field, F32),
            jax.ShapeDtypeStruct(field, F32),
            jax.ShapeDtypeStruct((DZ, nx, YL), F32),
        ],
        in_specs=[vmem] * len(kept),
        out_specs=[any_spec] * 4,
        scratch_shapes=[
            pltpu.VMEM(field, F32),
            pltpu.VMEM(field, F32),
            pltpu.VMEM(field, F32),
            pltpu.VMEM((DZ, nx, YL), F32),
            pltpu.SemaphoreType.DMA((3, CHUNKS)),
            pltpu.SemaphoreType.DMA(()),
        ],
        compiler_params=pltpu.CompilerParams(vmem_limit_bytes=24 << 20),
        name="finish",
    )(*mid)
    return e, h, j, jnp.transpose(grad, (1, 0, 2))


def solution(mesh):
    field = P(None, "gx", None, "gy")
    cell = P("gx", None, "gy")
    return jax.shard_map(
        functools.partial(body, mesh.shape["gx"], mesh.shape["gy"]),
        mesh=mesh,
        in_specs=(field, field, field, cell, P(), field, P()),
        out_specs=(field, field, field, cell),
        check_vma=False,
    )
```
